256 devices in a mesh: rep: 2 (over core), ctx: 32 (over y, z), tp: 4 (over x).
Axes of the slice: x: 4, y: 4, z: 8, core: 2. Of those that a mesh axis runs over, the one named last changes fastest.
Arguments:
- q_mr: bfloat16 [16384, 8192], P(('rep', 'ctx'), 'tp'), parts along dimension 0, may hold values from -6 to 6
- k_mr: bfloat16 [16384, 8192], P(('rep', 'ctx'), 'tp'), parts along dimension 0, may hold values from -6 to 6
- v_mr: bfloat16 [16384, 8192], P(('rep', 'ctx'), 'tp'), parts along dimension 0, may hold values from -6 to 6
- q_li: bfloat16 [16384, 8192], P(('rep', 'ctx'), 'tp'), parts along dimension 0, may hold values from -6 to 6
- k_li: bfloat16 [16384, 8192], P(('rep', 'ctx'), 'tp'), parts along dimension 0, may hold values from -6 to 6
- mr_taps: bfloat16 [512, 128], P('tp'), may hold values from -0.5 to 0.5
- li_rate: float32 [512, 16], P('tp'), may hold values from 0 to 0.0625, as said below
- li_residue: float32 [512, 16], P('tp'), may hold values from -1.5 to 1.5
Outputs:
- mr_out: bfloat16 [16384, 8192], P(('rep', 'ctx'), 'tp'), parts along dimension 0
- li_out: bfloat16 [16384, 8192], P(('rep', 'ctx'), 'tp'), parts along dimension 0
The draws below stay inside these ranges and needn't reach their ends.
There are 2 independent parts, one for each index of `rep`. The reference program is written for one: setup_inputs(seed, part) draws one part's arguments, and reference() takes and returns one part's arrays. A program takes and returns all parts, laid end to end along the dimension named above; an argument that names none is the same for every part. Nothing has to cross between parts.
Inputs may be any that keep to these rules, and one draw needn't show every extreme that they name: `li_rate`: positive decay rates per position.
All inputs are finite; a program needn't handle non-finite values.
Results may differ from the reference program's by a relative error of at most 0.013.
Values may be sent and summed in bfloat16 or wider, within the bound.
A program may use at most 128 MiB of HBM per device.

```python
import jax
import jax.numpy as jnp
from jax import lax

D = 8192
GROUPS = 512
POLES = 16
MR_LEN = 128
TOK_DEV = 256
SEQ = 8192
N_CTX = 32


def draw_li_rate(key, part):
    key_mix, key_slow, key_fast = jax.random.split(jax.random.fold_in(key, 17), 3)
    chooser = jax.random.randint(key_mix, (GROUPS, POLES), 0, 10)
    slow_u = jax.random.uniform(key_slow, (GROUPS, POLES), jnp.float32)
    fast_u = jax.random.uniform(key_fast, (GROUPS, POLES), jnp.float32)
    edge_rate = 2.3 / SEQ
    low_rate = 0.3 / SEQ
    cut_level = 5
    slow_rate = low_rate * jnp.exp(slow_u * jnp.log(edge_rate / low_rate))
    fast_rate = edge_rate * jnp.exp(fast_u * jnp.log(0.0625 / edge_rate))
    return jnp.where(chooser < cut_level, slow_rate, fast_rate).astype(jnp.float32)


def level_of(stream_key, extent, cuts, low, largest):
    def one(axis_at, parts):
        steps = jax.random.uniform(jax.random.fold_in(jax.random.fold_in(stream_key, 6), axis_at), (parts,), jnp.float32, low / len(cuts), largest / len(cuts))
        return jnp.repeat(jnp.exp(steps), extent[axis_at] // parts).reshape((-1,) + (1,) * (len(extent) - axis_at - 1))

    factor_of = one(*cuts[0])
    for cut in cuts[1:]:
        factor_of = factor_of * one(*cut)
    return factor_of


def centred(own_key, dims, spread, reach, cuts=(), held_as=jnp.bfloat16):
    entries = jax.random.normal(own_key, dims, jnp.float32) * spread
    if len(cuts) > 0:
        entries = level_of(own_key, dims, cuts, -0.22, 0.18) * entries
    return jnp.clip(entries, min=-reach, max=reach).astype(held_as)


def setup_inputs(seed: int = 0, part: int = 0) -> dict:
    splits = jax.random.split(jax.random.key(seed), 9)
    own_keys = jax.random.split(jax.random.fold_in(splits[8], part), 9)
    q_mr = centred(own_keys[0], (SEQ, D), 1.0, 6.0, ((0, 32), (1, 4)))
    k_mr = centred(own_keys[1], (SEQ, D), 1.0, 6.0, ((0, 32), (1, 4)))
    v_mr = centred(own_keys[2], (SEQ, D), 1.0, 6.0, ((0, 32), (1, 4)))
    q_li = centred(own_keys[3], (SEQ, D), 1.0, 6.0, ((0, 32), (1, 4)))
    k_li = centred(own_keys[4], (SEQ, D), 1.0, 6.0, ((0, 32), (1, 4)))
    mr_taps = centred(splits[5], (GROUPS, MR_LEN), MR_LEN ** -0.5, 0.5, ((0, 4),))
    li_rate = draw_li_rate(jax.random.fold_in(splits[8], 71), part)
    li_residue = centred(splits[7], (GROUPS, POLES), 0.25, 1.5, ((0, 4),), jnp.float32)
    return dict(q_mr=q_mr, k_mr=k_mr, v_mr=v_mr, q_li=q_li, k_li=k_li, mr_taps=mr_taps, li_rate=li_rate, li_residue=li_residue)


highest = lax.Precision.HIGHEST

def modal_tables(li_rate, li_residue, block_len):
    positions = jnp.arange(block_len).astype(jnp.float32)
    rate_col = li_rate[:, :, None]
    res_scale = li_residue * jnp.sqrt(-jnp.expm1(-2.0 * li_rate))
    li_taps = jnp.einsum('gp,gpt->gt', res_scale, jnp.exp(-rate_col * positions), precision=highest)
    end_w = jnp.exp(-rate_col * (block_len - 1.0 - positions))
    carry_w = res_scale[:, :, None] * jnp.exp(-rate_col * (positions + 1.0))
    block_decay = jnp.exp(-li_rate * block_len)
    return (li_taps, end_w, carry_w, block_decay)

def lower_toeplitz(li_taps):
    tap_len = li_taps.shape[1]
    lag_index = jnp.arange(tap_len)[:, None] - jnp.arange(tap_len)[None, :]
    gathered = li_taps[:, jnp.clip(lag_index, 0, tap_len - 1)]
    return jnp.where(lag_index >= 0, gathered, jnp.zeros_like(gathered))

def reference(q_mr, k_mr, v_mr, q_li, k_li, mr_taps, li_rate, li_residue):
    group_width = D // GROUPS
    block_len = TOK_DEV
    u_mr = (k_mr * v_mr).astype(jnp.bfloat16)
    padded = jnp.concatenate([jnp.zeros((MR_LEN - 1, D), jnp.bfloat16), u_mr], axis=0)
    lag_index = jnp.arange(block_len)[:, None] + (MR_LEN - 1) - jnp.arange(block_len + MR_LEN - 1)[None, :]
    tap_values = mr_taps.astype(jnp.float32)[:, jnp.clip(lag_index, 0, MR_LEN - 1)]
    inside = (lag_index >= 0) & (lag_index < MR_LEN)
    mr_table = jnp.where(inside, tap_values, jnp.zeros_like(tap_values))

    def mr_block(block_index):
        start_row = (block_index * block_len).astype(jnp.int32)
        block_rows = lax.dynamic_slice_in_dim(padded, start_row, block_len + MR_LEN - 1, 0)
        block_rows = block_rows.astype(jnp.float32).reshape(block_len + MR_LEN - 1, GROUPS, group_width)
        return jnp.einsum('gts,sgc->tgc', mr_table, block_rows, precision=highest).reshape(block_len, D)
    conv_mr = lax.map(mr_block, jnp.arange(N_CTX).astype(jnp.int32)).reshape(SEQ, D)
    mr_out = (q_mr * conv_mr).astype(jnp.bfloat16)
    u_li = (k_li * mr_out).astype(jnp.bfloat16)
    li_taps, end_w, carry_w, block_decay = modal_tables(li_rate, li_residue, block_len)
    li_table = lower_toeplitz(li_taps)
    blocked = u_li.reshape(N_CTX, block_len, GROUPS, group_width)

    def li_step(carried, block_rows):
        block_rows = block_rows.astype(jnp.float32)
        near_part = jnp.einsum('gts,sgc->tgc', li_table, block_rows, precision=highest)
        far_part = jnp.einsum('gpt,gpc->tgc', carry_w, carried, precision=highest)
        local_state = jnp.einsum('gps,sgc->gpc', end_w, block_rows, precision=highest)
        updated = block_decay[:, :, None] * carried + local_state
        return (updated, (near_part + far_part).reshape(block_len, D))
    initial = jnp.zeros((GROUPS, POLES, group_width), jnp.float32)
    _, conv_li = lax.scan(li_step, initial, blocked)
    li_out = (q_li * conv_li.reshape(SEQ, D)).astype(jnp.bfloat16)
    return (mr_out, li_out)
```

```python
import functools

import jax
import jax.numpy as jnp
from jax import lax
from jax.experimental import pallas as pl
from jax.experimental.pallas import tpu as pltpu
from jax.sharding import PartitionSpec as P

MESH = pl.DeviceIdType.MESH
HIGHEST = lax.Precision.HIGHEST
F32 = jnp.float32
BF16 = jnp.bfloat16
LANES = 128
HALF = 128
CHUNK_BLOCKS = 2
NEAR_FIRST = 8


def one_minus_exp_neg(x):
    s = x * (1.0 - x * (1 / 2) * (1.0 - x * (1 / 3) * (1.0 - x * (1 / 4) * (1.0 - x * (1 / 5) * (1.0 - x * (1 / 6) * (1.0 - x * (1 / 7)))))))
    return jnp.where(x < 0.25, s, 1.0 - jnp.exp(-x))


def iota(shape, dim):
    return lax.broadcasted_iota(jnp.int32, shape, dim)


def kernel(
    n, width, poles,
    q_h, k_h, v_h, ql_h, kl_h, taps_r, rate_r, resid_r,
    mr_h, li_h,
    kb, vb, qb, qlb, klb, u_ext, w_ext, mrb, lib, t_mr, t_li, end_w, carry_w, near,
    s_loc, s_in, e_out, e_loc, tap_row, base0, base1, rate_l, res_l, dec,
    in_sem, out_sem, h_send, h_recv, s_send, s_recv, e_send, e_recv,
):
    me = lax.axis_index("ctx")
    right = lax.rem(me + 1, n)
    rows, channels = kb.shape
    groups = channels // width
    blocks = channels // LANES
    gb = LANES // width
    chunks = blocks // CHUNK_BLOCKS
    cw = CHUNK_BLOCKS * LANES

    def inp(src, dst, i):
        return pltpu.make_async_copy(src, dst, in_sem.at[i])

    top, low = pl.ds(0, HALF), pl.ds(HALF, HALF)
    loads = [
        inp(k_h.at[low], kb.at[low], 0),
        inp(v_h.at[low], vb.at[low], 1),
        inp(k_h.at[top], kb.at[top], 2),
        inp(v_h.at[top], vb.at[top], 3),
        inp(q_h, qb, 4),
        inp(kl_h, klb, 5),
        inp(ql_h, qlb, 6),
    ]
    for copy in loads:
        copy.start()

    barrier = pltpu.get_barrier_semaphore()

    @pl.loop(1, n)
    def _(i):
        pl.semaphore_signal(barrier, inc=1, device_id={"ctx": lax.rem(me + i, n)}, device_id_type=MESH)

    loads[0].wait()
    loads[1].wait()
    u_ext[2 * HALF :, :] = kb[HALF:, :] * vb[HALF:, :]
    pl.semaphore_wait(barrier, n - 1)

    def halo(c):
        lanes = pl.ds(pl.multiple_of(c * cw, cw), cw)
        return pltpu.make_async_remote_copy(
            src_ref=u_ext.at[pl.ds(2 * HALF, HALF), lanes],
            dst_ref=u_ext.at[pl.ds(0, HALF), lanes],
            send_sem=h_send.at[c],
            recv_sem=h_recv.at[c],
            device_id={"ctx": right},
            device_id_type=MESH,
        )

    @pl.loop(0, chunks)
    def _(c):
        halo(c).start()

    t_i, x_i = iota((HALF, LANES), 0), iota((HALF, LANES), 1)
    flip = (t_i == ((LANES - x_i) & (LANES - 1))).astype(BF16)
    tap_row[...] = jnp.dot(taps_r[...], flip, preferred_element_type=F32)

    def circulant(ref, g):
        row = jnp.broadcast_to(ref[pl.ds(g, 1), :], (HALF, LANES))
        return pltpu.roll(row, 0, 1, stride=1, stride_axis=0)

    @pl.loop(0, groups)
    def _(g):
        at = pl.ds(pl.multiple_of(g * HALF, HALF), HALF)
        circ = circulant(tap_row, g)
        t_mr[at, 0:LANES] = jnp.where(x_i > t_i, circ, 0.0).astype(BF16)
        t_mr[at, LANES:] = jnp.where(x_i > t_i, 0.0, circ).astype(BF16)

    loads[2].wait()
    loads[3].wait()
    u_ext[HALF : 2 * HALF, :] = kb[:HALF, :] * vb[:HALF, :]
    w_ext[0:HALF, :] = jnp.zeros((HALF, channels), BF16)

    rate = rate_r[...]
    scale = resid_r[...] * jnp.sqrt(one_minus_exp_neg(2.0 * rate))
    far_scale = scale * jnp.exp(-float(HALF) * rate)
    lag = ((LANES - iota((groups, LANES), 1)) & (LANES - 1)).astype(F32)
    acc0 = jnp.zeros((groups, LANES), F32)
    acc1 = jnp.zeros((groups, LANES), F32)
    for p in range(poles):
        decay = jnp.exp(-rate[:, p : p + 1] * lag)
        acc0 = acc0 + scale[:, p : p + 1] * decay
        acc1 = acc1 + far_scale[:, p : p + 1] * decay
    base0[...] = acc0
    base1[...] = acc1

    pick = (iota((poles, groups * poles), 1) % poles == iota((poles, groups * poles), 0)).astype(F32)
    mine = iota((groups, groups * poles), 1) // poles == iota((groups, groups * poles), 0)

    def on_lanes(x):
        wide = jnp.dot(x, pick, precision=HIGHEST, preferred_element_type=F32)
        return jnp.sum(jnp.where(mine, wide, 0.0), axis=0, keepdims=True)

    rate_l[...] = on_lanes(rate)
    res_l[...] = on_lanes(scale)
    spread = (iota((groups, channels), 1) // width == iota((groups, channels), 0)).astype(F32)
    rate_t = lax.dot_general(rate, spread, (((0,), (0,)), ((), ())), precision=HIGHEST, preferred_element_type=F32)
    dec[...] = jnp.exp(-float(rows) * rate_t)

    pos = iota((rows, LANES), 0).astype(F32)

    @pl.loop(0, blocks)
    def _(j):
        lanes = pl.ds(pl.multiple_of(j * LANES, LANES), LANES)
        r = rate_l[:, lanes]
        carry_w[:, lanes] = (res_l[:, lanes] * jnp.exp(-r * (pos + 1.0))).astype(BF16)
        end_w[lanes, :] = jnp.exp(-r * (rows - 1.0 - pos)).T.astype(BF16)

    loads[4].wait()
    loads[5].wait()

    wide_g = (iota((HALF, 2 * LANES), 1) % LANES) // width
    one_g = iota((poles, LANES), 1) // width

    def chosen(res, which, size):
        out = res[0:size]
        for g in range(1, gb):
            out = jnp.where(which == g, res[g * size : (g + 1) * size], out)
        return out

    def piece(o):
        return pl.ds(pl.multiple_of(8 * lax.rem(o, 2), 8), 8), pl.ds(pl.multiple_of(LANES * (o // 2), LANES), LANES)

    def state_copy(o, frm):
        a, b = piece(o)
        return pltpu.make_async_remote_copy(
            src_ref=s_loc.at[a, b], dst_ref=s_in.at[frm], send_sem=s_send.at[o], recv_sem=s_recv.at[frm],
            device_id={"ctx": o}, device_id_type=MESH,
        )

    def mr_block(j):
        lanes = pl.ds(pl.multiple_of(j * LANES, LANES), LANES)
        at = pl.ds(pl.multiple_of(j * gb * HALF, gb * HALF), gb * HALF)
        rhs = jnp.concatenate([u_ext[0 : 2 * HALF, lanes], u_ext[HALF : 3 * HALF, lanes]], axis=1)
        res = jnp.dot(t_mr[at, :], rhs, preferred_element_type=F32)
        conv = chosen(res, wide_g, HALF)
        for b in range(2):
            part = pl.ds(b * HALF, HALF)
            out = (qb[part, lanes].astype(F32) * conv[:, b * LANES : (b + 1) * LANES]).astype(BF16)
            mrb[part, lanes] = out
            w_ext[pl.ds((b + 1) * HALF, HALF), lanes] = klb[part, lanes] * out
        st = jnp.dot(end_w[lanes, :], w_ext[HALF : 3 * HALF, lanes], preferred_element_type=F32)
        s_loc[:, lanes] = chosen(st, one_g, poles)
        for h in range(2):
            o = 2 * j + h

            @pl.when(o != me)
            def _():
                state_copy(o, me).start()

            @pl.when(o == me)
            def _():
                s_in[me] = s_loc[8 * h : 8 * h + 8, lanes]

    @pl.loop(0, chunks)
    def _(c):
        halo(c).wait_recv()

        @pl.when(me == 0)
        def _():
            lanes = pl.ds(pl.multiple_of(c * cw, cw), cw)
            u_ext[0:HALF, lanes] = jnp.zeros((HALF, cw), BF16)

        for i in range(CHUNK_BLOCKS):
            mr_block(c * CHUNK_BLOCKS + i)

    mr_store = pltpu.make_async_copy(mrb, mr_h, out_sem.at[0])
    mr_store.start()

    @pl.loop(0, groups)
    def _(g):
        at = pl.ds(pl.multiple_of(g * HALF, HALF), HALF)
        c0, c1 = circulant(base0, g), circulant(base1, g)
        t_li[at, 0:LANES] = jnp.where(x_i > t_i, c0, c1).astype(BF16)
        t_li[at, LANES:] = jnp.where(x_i > t_i, 0.0, c0).astype(BF16)

    def near_block(j):
        lanes = pl.ds(pl.multiple_of(j * LANES, LANES), LANES)
        at = pl.ds(pl.multiple_of(j * gb * HALF, gb * HALF), gb * HALF)
        rhs = jnp.concatenate([w_ext[0 : 2 * HALF, lanes], w_ext[HALF : 3 * HALF, lanes]], axis=1)
        res = jnp.dot(t_li[at, :], rhs, preferred_element_type=F32)
        conv = chosen(res, wide_g, HALF)
        near[0:HALF, lanes] = conv[:, :LANES]
        near[HALF:, lanes] = conv[:, LANES:]

    @pl.loop(0, NEAR_FIRST)
    def _(j):
        near_block(j)

    @pl.loop(1, n)
    def _(i):
        o = lax.rem(me + i, n)
        state_copy(me, o).wait_recv()

    my_a, my_b = piece(me)

    def enter_copy(owner, to):
        a, b = piece(owner)
        return pltpu.make_async_remote_copy(
            src_ref=e_out.at[to], dst_ref=e_loc.at[a, b], send_sem=e_send.at[to], recv_sem=e_recv.at[owner],
            device_id={"ctx": to}, device_id_type=MESH,
        )

    my_dec = dec[my_a, my_b]
    carried = jnp.zeros((8, LANES), F32)
    for b in range(n):
        e_out[b] = carried
        if b + 1 < n:
            carried = carried * my_dec + s_in[b]

    @pl.loop(1, n)
    def _(i):
        enter_copy(me, lax.rem(me + i, n)).start()

    e_loc[my_a, my_b] = e_out[me]

    @pl.loop(NEAR_FIRST, blocks)
    def _(j):
        near_block(j)

    loads[6].wait()

    @pl.loop(1, n)
    def _(i):
        enter_copy(lax.rem(me + i, n), me).wait_recv()

    row_g = iota((LANES, LANES), 0) // poles
    col_g = iota((LANES, LANES), 1) // width

    @pl.loop(0, blocks)
    def _(j):
        lanes = pl.ds(pl.multiple_of(j * LANES, LANES), LANES)
        e = e_loc[:, lanes]
        diag = jnp.where(row_g == col_g, jnp.concatenate([e] * gb, axis=0), 0.0).astype(BF16)
        far = jnp.dot(carry_w[:, lanes], diag, preferred_element_type=F32)
        lib[:, lanes] = (qlb[:, lanes].astype(F32) * (near[:, lanes] + far)).astype(BF16)

    li_store = pltpu.make_async_copy(lib, li_h, out_sem.at[1])
    li_store.start()

    @pl.loop(0, chunks)
    def _(c):
        halo(c).wait_send()

    @pl.loop(1, n)
    def _(i):
        o = lax.rem(me + i, n)
        state_copy(o, me).wait_send()
        enter_copy(me, o).wait_send()

    mr_store.wait()
    li_store.wait()


def body(n, q, k, v, ql, kl, taps, rate, resid):
    rows, channels = q.shape
    groups, poles = rate.shape
    width = channels // groups
    blocks = channels // LANES
    chunks = blocks // CHUNK_BLOCKS
    assert rows == 2 * HALF and taps.shape[1] == HALF and 2 * blocks == n and width == poles == 16
    dma = pltpu.SemaphoreType.DMA
    vm = pltpu.VMEM
    hbm = pl.BlockSpec(memory_space=pl.ANY)
    small = pl.BlockSpec(memory_space=pltpu.VMEM)
    full = vm((rows, channels), BF16)
    out = jax.ShapeDtypeStruct((rows, channels), BF16)
    return pl.pallas_call(
        functools.partial(kernel, n, width, poles),
        out_shape=(out, out),
        in_specs=[hbm] * 5 + [small] * 3,
        out_specs=(hbm, hbm),
        scratch_shapes=[
            full, full, full, full, full,
            vm((3 * HALF, channels), BF16), vm((3 * HALF, channels), BF16),
            full, full,
            vm((groups * HALF, 2 * LANES), BF16), vm((groups * HALF, 2 * LANES), BF16),
            vm((groups * poles, rows), BF16), vm((rows, groups * poles), BF16),
            vm((rows, channels), F32),
            vm((poles, channels), F32), vm((n, 8, LANES), F32), vm((n, 8, LANES), F32), vm((poles, channels), F32),
            vm((groups, LANES), F32), vm((groups, LANES), F32), vm((groups, LANES), F32),
            vm((1, groups * poles), F32), vm((1, groups * poles), F32), vm((poles, channels), F32),
            dma((7,)), dma((2,)), dma((chunks,)), dma((chunks,)), dma((n,)), dma((n,)), dma((n,)), dma((n,)),
        ],
        compiler_params=pltpu.CompilerParams(collective_id=0, has_side_effects=True, vmem_limit_bytes=60 << 20),
        cost_estimate=pl.CostEstimate(flops=4 * 10**9, bytes_accessed=8 << 20, transcendentals=0),
    )(q, k, v, ql, kl, taps, rate, resid)


def solution(mesh):
    rep_ctx = ("rep", "ctx")
    big = P(rep_ctx, "tp")
    return jax.shard_map(
        functools.partial(body, mesh.shape["ctx"]),
        mesh=mesh,
        in_specs=(big,) * 5 + (P("tp", None),) * 3,
        out_specs=(big, big),
        check_vma=False,
    )
```

```python
import functools

import jax
import jax.numpy as jnp
from jax import lax
from jax.experimental import pallas as pl
from jax.experimental.pallas import tpu as pltpu
from jax.sharding import PartitionSpec as P

MESH = pl.DeviceIdType.MESH
F32 = jnp.float32
BF16 = jnp.bfloat16
LANES = 128
TAPS = 128
STEP = 32
QUAD = LANES // STEP
CHUNK_BLOCKS = 2
EARLY = 4


def one_minus_exp_neg(x):
    s = x * (1.0 - x * (1 / 2) * (1.0 - x * (1 / 3) * (1.0 - x * (1 / 4) * (1.0 - x * (1 / 5) * (1.0 - x * (1 / 6) * (1.0 - x * (1 / 7)))))))
    return jnp.where(x < 0.25, s, 1.0 - jnp.exp(-x))


def iota(shape, dim):
    return lax.broadcasted_iota(jnp.int32, shape, dim)


def kernel(
    n, width, poles,
    q_h, k_h, v_h, ql_h, kl_h, taps_r, rate_r, resid_r,
    mr_h, li_h,
    kb, vb, qb, qlb, klb, u_ext, mrb, lib, t_mr, t_li, carry_w, near, s_part,
    s_loc, s_in, e_out, e_loc, tap_row, lag_row, scale_r, dec_step, dec_all,
    in_sem, out_sem, h_send, h_recv, s_send, s_recv, e_send, e_recv,
):
    me = lax.axis_index("ctx")
    right = lax.rem(me + 1, n)
    rows, channels = kb.shape
    groups = channels // width
    blocks = channels // LANES
    gb = LANES // width
    steps = rows // STEP
    window = TAPS + STEP
    chunks = blocks // CHUNK_BLOCKS
    cw = CHUNK_BLOCKS * LANES

    def inp(src, dst, i):
        return pltpu.make_async_copy(src, dst, in_sem.at[i])

    tail, head = pl.ds(rows - TAPS, TAPS), pl.ds(0, rows - TAPS)
    loads = [
        inp(k_h.at[tail], kb.at[tail], 0),
        inp(v_h.at[tail], vb.at[tail], 1),
        inp(k_h.at[head], kb.at[head], 2),
        inp(v_h.at[head], vb.at[head], 3),
        inp(q_h, qb, 4),
        inp(kl_h, klb, 5),
        inp(ql_h, qlb, 6),
    ]
    for copy in loads:
        copy.start()

    barrier = pltpu.get_barrier_semaphore()

    @pl.loop(1, n)
    def _(i):
        pl.semaphore_signal(barrier, inc=1, device_id={"ctx": lax.rem(me + i, n)}, device_id_type=MESH)

    def block(j):
        return pl.ds(pl.multiple_of(j * LANES, LANES), LANES)

    rate_t = rate_r[...]
    scale_t = resid_r[...] * jnp.sqrt(one_minus_exp_neg(2.0 * rate_t))
    scale_r[...] = scale_t
    lane1 = iota((1, LANES), 1)
    flip = (iota((TAPS, LANES), 0) == ((LANES - iota((TAPS, LANES), 1)) & (LANES - 1))).astype(BF16)
    tap_row[...] = jnp.dot(taps_r[...], flip, preferred_element_type=F32)

    rate = rate_t.T
    scale = scale_t.T
    lag = ((STEP - iota((groups, LANES), 1) % STEP) % STEP).astype(F32)
    acc = jnp.zeros((groups, LANES), F32)
    for p in range(poles):
        acc = acc + scale[:, p : p + 1] * jnp.exp(-rate[:, p : p + 1] * lag)
    lag_row[...] = acc

    x_i = iota((8, LANES), 1)
    t_i = iota((8, LANES), 0)
    lane_p = iota((poles, LANES), 1)
    pole_p = iota((poles, LANES), 0)
    seg, off = lane1 // STEP, lane1 % STEP

    def skewed(row):
        first = pltpu.roll(jnp.broadcast_to(row, (8, LANES)), 0, 1, stride=1, stride_axis=0)
        return [first] + [pltpu.roll(first, 8 * m, 1) for m in range(1, STEP // 8)]

    def tables(j):
        lanes = block(j)
        for g in range(gb):
            at = pl.ds(pl.multiple_of((j * gb + g) * STEP, STEP), STEP)
            parts = skewed(tap_row[pl.ds(j * gb + g, 1), :])
            far = [jnp.where(x_i > t_i + 8 * m, part, 0.0) for m, part in enumerate(parts)]
            own = [jnp.where(x_i > t_i + 8 * m, 0.0, part) for m, part in enumerate(parts)]
            t_mr[at, 0:LANES] = jnp.concatenate(far, axis=0).astype(BF16)
            t_mr[at, LANES:] = jnp.concatenate(own, axis=0).astype(BF16)
        for h in range(gb // QUAD):
            base = pl.multiple_of(j * 2 * (STEP + poles), 16)
            quad = (j * gb) + h * QUAD
            row = jnp.zeros((1, LANES), F32)
            for r in range(QUAD):
                here = ((off == 0) & (seg == r)) | ((off > 0) & (seg == (r - 1) % QUAD))
                row = jnp.where(here, lag_row[pl.ds(quad + r, 1), :], row)
            parts = skewed(row)
            own = [jnp.where((x_i % STEP) > t_i + 8 * m, 0.0, part) for m, part in enumerate(parts)]
            t_li[pl.ds(base + h * STEP, STEP), :] = jnp.concatenate(own, axis=0).astype(BF16)
            r_q = jnp.take_along_axis(rate_r[...], quad + lane_p // STEP, axis=1)
            w = jnp.exp(-r_q * (STEP - 1 - lane_p % STEP).astype(F32))
            t_li[pl.ds(base + 2 * STEP + h * poles, poles), :] = w.astype(BF16)
        index = j * gb + lane_p // width
        r_c = jnp.take_along_axis(rate_r[...], index, axis=1)
        s_c = jnp.take_along_axis(scale_r[...], index, axis=1)
        dec_step[:, lanes] = jnp.exp(-float(STEP) * r_c)
        dec_all[:, lanes] = jnp.exp(-float(rows) * r_c)
        diag = pole_p == lane_p % poles
        r_l = jnp.sum(jnp.where(diag, r_c, 0.0), axis=0, keepdims=True)
        s_l = jnp.sum(jnp.where(diag, s_c, 0.0), axis=0, keepdims=True)
        carry_w[:, lanes] = (s_l * jnp.exp(-r_l * (iota((STEP, LANES), 0) + 1).astype(F32))).astype(BF16)

    loads[0].wait()
    loads[1].wait()
    u_ext[rows:, :] = kb[rows - TAPS :, :] * vb[rows - TAPS :, :]

    @pl.loop(0, EARLY)
    def _(j):
        tables(j)

    pl.semaphore_wait(barrier, n - 1)

    def halo(c):
        lanes = pl.ds(pl.multiple_of(c * cw, cw), cw)
        return pltpu.make_async_remote_copy(
            src_ref=u_ext.at[pl.ds(rows, TAPS), lanes],
            dst_ref=u_ext.at[pl.ds(0, TAPS), lanes],
            send_sem=h_send.at[c],
            recv_sem=h_recv.at[c],
            device_id={"ctx": right},
            device_id_type=MESH,
        )

    @pl.loop(0, chunks)
    def _(c):
        halo(c).start()

    @pl.loop(EARLY, blocks)
    def _(j):
        tables(j)

    loads[2].wait()
    loads[3].wait()
    u_ext[TAPS:rows, :] = kb[: rows - TAPS, :] * vb[: rows - TAPS, :]
    loads[4].wait()
    loads[5].wait()

    group_2 = (iota((STEP, 2 * LANES), 1) % LANES) // width
    left_t = (iota((STEP, 2 * LANES), 1) % LANES) < LANES // 2
    left_p = (iota((poles, 2 * LANES), 1) % LANES) < LANES // 2
    quad_g = (iota((STEP, LANES), 1) // width) % QUAD
    pole_g = iota((poles, LANES), 1) // width

    def piece(o):
        return pl.ds(pl.multiple_of(8 * lax.rem(o, 2), 8), 8), block(o // 2)

    def state_copy(o, frm):
        a, b = piece(o)
        return pltpu.make_async_remote_copy(
            src_ref=s_loc.at[a, b], dst_ref=s_in.at[frm], send_sem=s_send.at[o], recv_sem=s_recv.at[frm],
            device_id={"ctx": o}, device_id_type=MESH,
        )

    def mix(j):
        lanes = block(j)
        at = pl.ds(pl.multiple_of(j * gb * STEP, gb * STEP), gb * STEP)
        li_at = pl.ds(pl.multiple_of(j * 2 * (STEP + poles), 16), 2 * (STEP + poles))
        step_dec = dec_step[:, lanes]
        state = jnp.zeros((poles, LANES), F32)
        for p in range(steps // 2):
            first = 2 * p * STEP
            rhs = jnp.concatenate([u_ext[first : first + window, lanes], u_ext[first + STEP : first + STEP + window, lanes]], axis=1)
            res = jnp.dot(t_mr[at, 0:window], rhs, preferred_element_type=F32)
            conv = res[0:STEP]
            for g in range(1, gb):
                conv = jnp.where(group_2 == g, res[g * STEP : (g + 1) * STEP], conv)
            diag = []
            for b in range(2):
                part = pl.ds(first + b * STEP, STEP)
                out = (qb[part, lanes].astype(F32) * conv[:, b * LANES : (b + 1) * LANES]).astype(BF16)
                mrb[part, lanes] = out
                u_li = klb[part, lanes] * out
                diag.append(jnp.concatenate([jnp.where(quad_g == r, u_li, jnp.zeros_like(u_li)) for r in range(QUAD)], axis=0))
            res = jnp.dot(t_li[li_at, :], jnp.concatenate(diag, axis=1), preferred_element_type=F32)
            own = jnp.where(left_t, res[0:STEP], res[STEP : 2 * STEP])
            ends = jnp.where(left_p, res[2 * STEP : 2 * STEP + poles], res[2 * STEP + poles :])
            for b in range(2):
                a = 2 * p + b
                near[pl.ds(a * STEP, STEP), lanes] = own[:, b * LANES : (b + 1) * LANES]
                s_part[a, :, lanes] = state
                state = state * step_dec + ends[:, b * LANES : (b + 1) * LANES]
        s_loc[:, lanes] = state
        for h in range(2):
            o = 2 * j + h

            @pl.when(o != me)
            def _():
                state_copy(o, me).start()

            @pl.when(o == me)
            def _():
                s_in[me] = s_loc[8 * h : 8 * h + 8, lanes]

    @pl.loop(0, chunks)
    def _(c):
        halo(c).wait_recv()

        @pl.when(me == 0)
        def _():
            lanes = pl.ds(pl.multiple_of(c * cw, cw), cw)
            u_ext[0:TAPS, lanes] = jnp.zeros((TAPS, cw), BF16)

        for i in range(CHUNK_BLOCKS):
            mix(c * CHUNK_BLOCKS + i)

    mr_store = pltpu.make_async_copy(mrb, mr_h, out_sem.at[0])
    mr_store.start()

    @pl.loop(1, n)
    def _(i):
        o = lax.rem(me + i, n)
        state_copy(me, o).wait_recv()

    my_a, my_b = piece(me)

    def enter_copy(owner, to):
        a, b = piece(owner)
        return pltpu.make_async_remote_copy(
            src_ref=e_out.at[to], dst_ref=e_loc.at[a, b], send_sem=e_send.at[to], recv_sem=e_recv.at[owner],
            device_id={"ctx": to}, device_id_type=MESH,
        )

    my_dec = dec_all[my_a, my_b]
    carried = jnp.zeros((8, LANES), F32)
    for b in range(n):
        e_out[b] = carried
        if b + 1 < n:
            carried = carried * my_dec + s_in[b]

    @pl.loop(1, n)
    def _(i):
        enter_copy(me, lax.rem(me + i, n)).start()

    e_loc[my_a, my_b] = e_out[me]
    loads[6].wait()

    @pl.loop(1, n)
    def _(i):
        enter_copy(lax.rem(me + i, n), me).wait_recv()

    @pl.loop(0, blocks)
    def _(j):
        lanes = block(j)
        e = e_loc[:, lanes]
        step_dec = dec_step[:, lanes]
        weights = carry_w[:, lanes]
        for p in range(steps // 2):
            diag = []
            for b in range(2):
                state = (s_part[2 * p + b, :, lanes] + e).astype(BF16)
                diag.append(jnp.concatenate([jnp.where(pole_g == g, state, jnp.zeros_like(state)) for g in range(gb)], axis=0))
                e = e * step_dec
            far = jnp.dot(weights, jnp.concatenate(diag, axis=1), preferred_element_type=F32)
            for b in range(2):
                part = pl.ds((2 * p + b) * STEP, STEP)
                conv = near[part, lanes] + far[:, b * LANES : (b + 1) * LANES]
                lib[part, lanes] = (qlb[part, lanes].astype(F32) * conv).astype(BF16)

    li_store = pltpu.make_async_copy(lib, li_h, out_sem.at[1])
    li_store.start()

    @pl.loop(0, chunks)
    def _(c):
        halo(c).wait_send()

    @pl.loop(1, n)
    def _(i):
        o = lax.rem(me + i, n)
        state_copy(o, me).wait_send()
        enter_copy(me, o).wait_send()

    mr_store.wait()
    li_store.wait()


def body(n, q, k, v, ql, kl, taps, rate, resid):
    rows, channels = q.shape
    groups, poles = rate.shape
    width = channels // groups
    blocks = channels // LANES
    chunks = blocks // CHUNK_BLOCKS
    assert taps.shape[1] == TAPS and 2 * blocks == n and width == poles == 16
    dma = pltpu.SemaphoreType.DMA
    vm = pltpu.VMEM
    hbm = pl.BlockSpec(memory_space=pl.ANY)
    small = pl.BlockSpec(memory_space=pltpu.VMEM)
    full = vm((rows, channels), BF16)
    out = jax.ShapeDtypeStruct((rows, channels), BF16)
    states = vm((poles, channels), F32)
    return pl.pallas_call(
        functools.partial(kernel, n, width, poles),
        out_shape=(out, out),
        in_specs=[hbm] * 5 + [small] * 3,
        out_specs=(hbm, hbm),
        scratch_shapes=[
            full, full, full, full, full,
            vm((TAPS + rows, channels), BF16),
            full, full,
            vm((groups * STEP, 2 * LANES), BF16),
            vm((blocks * 2 * (STEP + poles), LANES), BF16),
            vm((STEP, groups * poles), BF16),
            vm((rows, channels), F32),
            vm((rows // STEP, poles, channels), F32),
            states, vm((n, 8, LANES), F32), vm((n, 8, LANES), F32), states,
            vm((groups, LANES), F32), vm((groups, LANES), F32), vm((poles, groups), F32), states, states,
            dma((7,)), dma((2,)), dma((chunks,)), dma((chunks,)), dma((n,)), dma((n,)), dma((n,)), dma((n,)),
        ],
        compiler_params=pltpu.CompilerParams(collective_id=0, has_side_effects=True, vmem_limit_bytes=60 << 20),
        cost_estimate=pl.CostEstimate(flops=4 * 10**9, bytes_accessed=8 << 20, transcendentals=0),
    )(q, k, v, ql, kl, taps, rate.T, resid.T)


def solution(mesh):
    rep_ctx = ("rep", "ctx")
    big = P(rep_ctx, "tp")
    return jax.shard_map(
        functools.partial(body, mesh.shape["ctx"]),
        mesh=mesh,
        in_specs=(big,) * 5 + (P("tp", None),) * 3,
        out_specs=(big, big),
        check_vma=False,
    )
```

```python
import functools

import jax
import jax.numpy as jnp
from jax import lax
from jax.experimental import pallas as pl
from jax.experimental.pallas import tpu as pltpu
from jax.sharding import PartitionSpec as P

MESH = pl.DeviceIdType.MESH
F32 = jnp.float32
BF16 = jnp.bfloat16
LANES = 128
TAPS = 128
STEP = 32
QUAD = LANES // STEP
CHUNK_BLOCKS = 2


def one_minus_exp_neg(x):
    s = x * (1.0 - x * (1 / 2) * (1.0 - x * (1 / 3) * (1.0 - x * (1 / 4) * (1.0 - x * (1 / 5) * (1.0 - x * (1 / 6) * (1.0 - x * (1 / 7)))))))
    return jnp.where(x < 0.25, s, 1.0 - jnp.exp(-x))


def iota(shape, dim):
    return lax.broadcasted_iota(jnp.int32, shape, dim)


def kernel(
    n, width, poles,
    q_h, k_h, v_h, ql_h, kl_h, taps_h, rate_h, resid_h,
    mr_h, li_h,
    kb, vb, qb, qlb, klb, taps_r, rate_r, resid_r, u_ext, t_mr, t_li, carry_w, near, s_part,
    s_loc, s_in, e_out, e_loc, tap_row, lag_row, scale_r, dec_step, dec_all,
    in_sem, h_send, h_recv, s_send, s_recv, e_send, e_recv,
):
    me = lax.axis_index("ctx")
    right = lax.rem(me + 1, n)
    rows, channels = kb.shape
    groups = channels // width
    blocks = channels // LANES
    gb = LANES // width
    steps = rows // STEP
    window = TAPS + STEP
    chunks = blocks // CHUNK_BLOCKS
    cw = CHUNK_BLOCKS * LANES

    def inp(src, dst, i):
        return pltpu.make_async_copy(src, dst, in_sem.at[i])

    tail, head = pl.ds(rows - TAPS, TAPS), pl.ds(0, rows - TAPS)
    loads = [
        inp(k_h.at[tail], kb.at[tail], 0),
        inp(v_h.at[tail], vb.at[tail], 1),
        inp(k_h.at[head], kb.at[head], 2),
        inp(v_h.at[head], vb.at[head], 3),
        inp(taps_h, taps_r, 7),
        inp(rate_h, rate_r, 8),
        inp(resid_h, resid_r, 9),
        inp(q_h, qb, 4),
        inp(kl_h, klb, 5),
        inp(ql_h, qlb, 6),
    ]
    for copy in loads:
        copy.start()

    barrier = pltpu.get_barrier_semaphore()

    @pl.loop(1, n)
    def _(i):
        pl.semaphore_signal(barrier, inc=1, device_id={"ctx": lax.rem(me + i, n)}, device_id_type=MESH)

    def block(j):
        return pl.ds(pl.multiple_of(j * LANES, LANES), LANES)

    loads[0].wait()
    loads[1].wait()
    u_ext[rows:, :] = kb[rows - TAPS :, :] * vb[rows - TAPS :, :]

    pl.semaphore_wait(barrier, n - 1)

    def halo(c):
        lanes = pl.ds(pl.multiple_of(c * cw, cw), cw)
        return pltpu.make_async_remote_copy(
            src_ref=u_ext.at[pl.ds(rows, TAPS), lanes],
            dst_ref=u_ext.at[pl.ds(0, TAPS), lanes],
            send_sem=h_send,
            recv_sem=h_recv.at[c],
            device_id={"ctx": right},
            device_id_type=MESH,
        )

    @pl.loop(0, chunks)
    def _(c):
        halo(c).start()

    for i in (4, 5, 6):
        loads[i].wait()

    rate_t = rate_r[...]
    scale_t = resid_r[...] * jnp.sqrt(one_minus_exp_neg(2.0 * rate_t))
    scale_r[...] = scale_t
    lane1 = iota((1, LANES), 1)
    flip = (iota((TAPS, LANES), 0) == ((LANES - iota((TAPS, LANES), 1)) & (LANES - 1))).astype(BF16)
    tap_row[...] = jnp.dot(taps_r[...], flip, preferred_element_type=F32)

    rate = rate_t.T
    scale = scale_t.T
    lag = ((STEP - iota((groups, LANES), 1) % STEP) % STEP).astype(F32)
    acc = jnp.zeros((groups, LANES), F32)
    for p in range(poles):
        acc = acc + scale[:, p : p + 1] * jnp.exp(-rate[:, p : p + 1] * lag)
    lag_row[...] = acc

    x_i = iota((8, LANES), 1)
    t_i = iota((8, LANES), 0)
    lane_p = iota((poles, LANES), 1)
    pole_p = iota((poles, LANES), 0)
    seg, off = lane1 // STEP, lane1 % STEP

    def skewed(row):
        first = pltpu.roll(jnp.broadcast_to(row, (8, LANES)), 0, 1, stride=1, stride_axis=0)
        return [first] + [pltpu.roll(first, 8 * m, 1) for m in range(1, STEP // 8)]

    def tables(j):
        lanes = block(j)
        for g in range(gb):
            at = pl.ds(pl.multiple_of((j * gb + g) * STEP, STEP), STEP)
            parts = skewed(tap_row[pl.ds(j * gb + g, 1), :])
            far = [jnp.where(x_i > t_i + 8 * m, part, 0.0) for m, part in enumerate(parts)]
            own = [jnp.where(x_i > t_i + 8 * m, 0.0, part) for m, part in enumerate(parts)]
            t_mr[at, 0:LANES] = jnp.concatenate(far, axis=0).astype(BF16)
            t_mr[at, LANES:] = jnp.concatenate(own, axis=0).astype(BF16)
        for h in range(gb // QUAD):
            base = pl.multiple_of(j * 2 * (STEP + poles), 16)
            quad = (j * gb) + h * QUAD
            row = jnp.zeros((1, LANES), F32)
            for r in range(QUAD):
                here = ((off == 0) & (seg == r)) | ((off > 0) & (seg == (r - 1) % QUAD))
                row = jnp.where(here, lag_row[pl.ds(quad + r, 1), :], row)
            parts = skewed(row)
            own = [jnp.where((x_i % STEP) > t_i + 8 * m, 0.0, part) for m, part in enumerate(parts)]
            t_li[pl.ds(base + h * STEP, STEP), :] = jnp.concatenate(own, axis=0).astype(BF16)
            r_q = jnp.take_along_axis(rate_r[...], quad + lane_p // STEP, axis=1)
            w = jnp.exp(-r_q * (STEP - 1 - lane_p % STEP).astype(F32))
            t_li[pl.ds(base + 2 * STEP + h * poles, poles), :] = w.astype(BF16)
        index = j * gb + lane_p // width
        r_c = jnp.take_along_axis(rate_r[...], index, axis=1)
        s_c = jnp.take_along_axis(scale_r[...], index, axis=1)
        dec_step[:, lanes] = jnp.exp(-float(STEP) * r_c)
        dec_all[:, lanes] = jnp.exp(-float(rows) * r_c)
        diag = pole_p == lane_p % poles
        r_l = jnp.sum(jnp.where(diag, r_c, 0.0), axis=0, keepdims=True)
        s_l = jnp.sum(jnp.where(diag, s_c, 0.0), axis=0, keepdims=True)
        carry_w[:, lanes] = (s_l * jnp.exp(-r_l * (iota((STEP, LANES), 0) + 1).astype(F32))).astype(BF16)

    @pl.loop(0, blocks)
    def _(j):
        tables(j)

    loads[2].wait()
    loads[3].wait()
    u_ext[TAPS:rows, :] = kb[: rows - TAPS, :] * vb[: rows - TAPS, :]
    loads[7].wait()
    loads[8].wait()

    group_w = (iota((STEP, rows // STEP * LANES), 1) % LANES) // width
    left_t = (iota((STEP, rows // STEP * LANES), 1) % LANES) < LANES // 2
    left_p = (iota((poles, rows // STEP * LANES), 1) % LANES) < LANES // 2
    quad_g = (iota((STEP, LANES), 1) // width) % QUAD
    pole_g = iota((poles, LANES), 1) // width

    def all_pieces(sem):
        pltpu.make_async_copy(e_out.at[pl.ds(0, n - 1)], s_in.at[pl.ds(0, n - 1)], sem).wait()

    def piece(o):
        return pl.ds(pl.multiple_of(8 * lax.rem(o, 2), 8), 8), block(o // 2)

    def state_copy(o, frm):
        a, b = piece(o)
        return pltpu.make_async_remote_copy(
            src_ref=s_loc.at[a, b], dst_ref=s_in.at[frm], send_sem=s_send, recv_sem=s_recv,
            device_id={"ctx": o}, device_id_type=MESH,
        )

    def short(j):
        lanes = block(j)
        at = pl.ds(pl.multiple_of(j * gb * STEP, gb * STEP), gb * STEP)
        rhs = jnp.concatenate([u_ext[a * STEP : a * STEP + window, lanes] for a in range(steps)], axis=1)
        res = jnp.dot(t_mr[at, 0:window], rhs, preferred_element_type=F32)
        conv = res[0:STEP]
        for g in range(1, gb):
            conv = jnp.where(group_w == g, res[g * STEP : (g + 1) * STEP], conv)
        diag = []
        for a in range(steps):
            part = pl.ds(a * STEP, STEP)
            out = (qb[part, lanes].astype(F32) * conv[:, a * LANES : (a + 1) * LANES]).astype(BF16)
            mr_h[part, lanes] = out
            u_li = klb[part, lanes] * out
            diag.append(jnp.concatenate([jnp.where(quad_g == r, u_li, jnp.zeros_like(u_li)) for r in range(QUAD)], axis=0))
        return jnp.concatenate(diag, axis=1)

    def long(j, diag):
        lanes = block(j)
        li_at = pl.ds(pl.multiple_of(j * 2 * (STEP + poles), 16), 2 * (STEP + poles))
        step_dec = dec_step[:, lanes]
        res = jnp.dot(t_li[li_at, :], diag, preferred_element_type=F32)
        own = jnp.where(left_t, res[0:STEP], res[STEP : 2 * STEP])
        ends = jnp.where(left_p, res[2 * STEP : 2 * STEP + poles], res[2 * STEP + poles :])
        state = None
        for a in range(steps):
            cut = slice(a * LANES, (a + 1) * LANES)
            near[pl.ds(a * STEP, STEP), lanes] = own[:, cut]
            if a == 0:
                state = ends[:, cut]
            else:
                s_part[a, :, lanes] = state
                state = state * step_dec + ends[:, cut]
        s_loc[:, lanes] = state

    def hand_out(j):
        lanes = block(j)
        for h in range(2):
            o = 2 * j + h

            @pl.when(o != me)
            def _():
                state_copy(o, me).start()

            @pl.when(o == me)
            def _():
                s_in[me] = s_loc[8 * h : 8 * h + 8, lanes]

    @pl.loop(0, chunks)
    def _(c):
        halo(c).wait_recv()

        @pl.when(me == 0)
        def _():
            lanes = pl.ds(pl.multiple_of(c * cw, cw), cw)
            u_ext[0:TAPS, lanes] = jnp.zeros((TAPS, cw), BF16)

        js = [c * CHUNK_BLOCKS + i for i in range(CHUNK_BLOCKS)]
        diags = [short(j) for j in js]
        for j, diag in zip(js, diags):
            long(j, diag)
        for j in js:
            hand_out(j)

    all_pieces(s_recv)

    my_a, my_b = piece(me)

    def enter_copy(owner, to):
        a, b = piece(owner)
        return pltpu.make_async_remote_copy(
            src_ref=e_out.at[to], dst_ref=e_loc.at[a, b], send_sem=e_send, recv_sem=e_recv,
            device_id={"ctx": to}, device_id_type=MESH,
        )

    my_dec = dec_all[my_a, my_b]
    carried = jnp.zeros((8, LANES), F32)
    for b in range(n):
        e_out[b] = carried
        if b + 1 < n:
            carried = carried * my_dec + s_in[b]

    @pl.loop(1, n)
    def _(i):
        enter_copy(me, lax.rem(me + i, n)).start()

    e_loc[my_a, my_b] = e_out[me]
    loads[9].wait()

    all_pieces(e_recv)

    def finish(j):
        lanes = block(j)
        e = e_loc[:, lanes]
        step_dec = dec_step[:, lanes]
        diag = []
        for a in range(steps):
            state = (s_part[a, :, lanes] + e if a else e).astype(BF16)
            diag.append(jnp.concatenate([jnp.where(pole_g == g, state, jnp.zeros_like(state)) for g in range(gb)], axis=0))
            e = e * step_dec
        far = jnp.dot(carry_w[:, lanes], jnp.concatenate(diag, axis=1), preferred_element_type=F32)
        for a in range(steps):
            part = pl.ds(a * STEP, STEP)
            conv = near[part, lanes] + far[:, a * LANES : (a + 1) * LANES]
            li_h[part, lanes] = (qlb[part, lanes].astype(F32) * conv).astype(BF16)

    @pl.loop(0, chunks)
    def _(c):
        for i in range(CHUNK_BLOCKS):
            finish(c * CHUNK_BLOCKS + i)

    pltpu.make_async_copy(u_ext.at[pl.ds(rows, TAPS)], u_ext.at[pl.ds(0, TAPS)], h_send).wait()
    all_pieces(s_send)
    all_pieces(e_send)


def body(n, q, k, v, ql, kl, taps, rate, resid):
    rows, channels = q.shape
    groups, poles = rate.shape
    width = channels // groups
    blocks = channels // LANES
    chunks = blocks // CHUNK_BLOCKS
    assert taps.shape[1] == TAPS and 2 * blocks == n and width == poles == 16
    dma = pltpu.SemaphoreType.DMA
    vm = pltpu.VMEM
    hbm = pl.BlockSpec(memory_space=pltpu.HBM)
    small = pl.BlockSpec(memory_space=pltpu.VMEM)
    full = vm((rows, channels), BF16)
    out = jax.ShapeDtypeStruct((rows, channels), BF16)
    states = vm((poles, channels), F32)
    return pl.pallas_call(
        functools.partial(kernel, n, width, poles),
        out_shape=(out, out),
        in_specs=[hbm] * 8,
        out_specs=(small, small),
        scratch_shapes=[
            full, full, full, full, full,
            vm(taps.shape, BF16), vm((poles, groups), F32), vm((poles, groups), F32),
            vm((TAPS + rows, channels), BF16),
            vm((groups * STEP, 2 * LANES), BF16),
            vm((blocks * 2 * (STEP + poles), LANES), BF16),
            vm((STEP, groups * poles), BF16),
            vm((rows, channels), F32),
            vm((rows // STEP, poles, channels), F32),
            states, vm((n, 8, LANES), F32), vm((n, 8, LANES), F32), states,
            vm((groups, LANES), F32), vm((groups, LANES), F32), vm((poles, groups), F32), states, states,
            dma((10,)), dma(()), dma((chunks,)), dma(()), dma(()), dma(()), dma(()),
        ],
        compiler_params=pltpu.CompilerParams(collective_id=0, has_side_effects=True, vmem_limit_bytes=28 << 20),
        cost_estimate=pl.CostEstimate(flops=4 * 10**9, bytes_accessed=8 << 20, transcendentals=0),
    )(*[pltpu.with_memory_space_constraint(x, pltpu.HBM) for x in (q, k, v, ql, kl, taps, rate.T, resid.T)])


def solution(mesh):
    rep_ctx = ("rep", "ctx")
    big = P(rep_ctx, "tp")
    return jax.shard_map(
        functools.partial(body, mesh.shape["ctx"]),
        mesh=mesh,
        in_specs=(big,) * 5 + (P("tp", None),) * 3,
        out_specs=(big, big),
        check_vma=False,
    )
```

```python
import functools

import jax
import jax.numpy as jnp
from jax import lax
from jax.experimental import pallas as pl
from jax.experimental.pallas import tpu as pltpu
from jax.sharding import PartitionSpec as P

MESH = pl.DeviceIdType.MESH
F32 = jnp.float32
BF16 = jnp.bfloat16
LANES = 128
TAPS = 128
STEP = 32
QUAD = LANES // STEP
STORES = 4
CHUNK_BLOCKS = 2
SCAN_LAG = 4


def one_minus_exp_neg(x):
    s = x * (1.0 - x * (1 / 2) * (1.0 - x * (1 / 3) * (1.0 - x * (1 / 4) * (1.0 - x * (1 / 5) * (1.0 - x * (1 / 6) * (1.0 - x * (1 / 7)))))))
    return jnp.where(x < 0.25, s, 1.0 - jnp.exp(-x))


def iota(shape, dim):
    return lax.broadcasted_iota(jnp.int32, shape, dim)


def kernel(
    n, width, poles,
    q_h, k_h, v_h, ql_h, kl_h, taps_h, rate_h, resid_h,
    mr_h, li_h,
    kb, vb, qb, qlb, klb, taps_r, rate_r, resid_r, u_ext, t_mr, t_li, carry_w, near, s_part,
    s_loc, s_in, e_out, e_loc, tap_row, lag_row, scale_r, dec_step, dec_all,
    known, in_sem, h_send, h_recv, s_send, s_recv, e_send, e_recv,
):
    me = lax.axis_index("ctx")
    right = lax.rem(me + 1, n)
    rows, channels = kb.shape
    groups = channels // width
    blocks = channels // LANES
    gb = LANES // width
    steps = rows // STEP
    window = TAPS + STEP
    chunks = blocks // CHUNK_BLOCKS
    cw = CHUNK_BLOCKS * LANES
    per_chunk = 2 * CHUNK_BLOCKS
    scan_at = me // per_chunk + SCAN_LAG

    def inp(src, dst, i):
        return pltpu.make_async_copy(src, dst, in_sem.at[i])

    tail, head = pl.ds(rows - TAPS, TAPS), pl.ds(0, rows - TAPS)
    loads = [
        inp(k_h.at[tail], kb.at[tail], 0),
        inp(v_h.at[tail], vb.at[tail], 1),
        inp(k_h.at[head], kb.at[head], 2),
        inp(v_h.at[head], vb.at[head], 3),
        inp(taps_h, taps_r, 7),
        inp(rate_h, rate_r, 8),
        inp(resid_h, resid_r, 9),
        inp(q_h, qb, 4),
        inp(kl_h, klb, 5),
        inp(ql_h, qlb, 6),
    ]
    for copy in loads:
        copy.start()

    barrier = pltpu.get_barrier_semaphore()

    def greet(sem, far):
        for i in (far, n - far):
            pl.semaphore_signal(sem, inc=1, device_id={"ctx": lax.rem(me + i, n)}, device_id_type=MESH)

    greet(barrier, 1)

    def widen(k):
        greet(known.at[k], 2**k)
        pl.semaphore_wait(known.at[k], 2)

    def block(j):
        return pl.ds(pl.multiple_of(j * LANES, LANES), LANES)

    loads[0].wait()
    loads[1].wait()
    u_ext[rows:, :] = kb[rows - TAPS :, :] * vb[rows - TAPS :, :]

    pl.semaphore_wait(barrier, 2)

    def halo(c):
        lanes = pl.ds(pl.multiple_of(c * cw, cw), cw)
        return pltpu.make_async_remote_copy(
            src_ref=u_ext.at[pl.ds(rows, TAPS), lanes],
            dst_ref=u_ext.at[pl.ds(0, TAPS), lanes],
            send_sem=h_send,
            recv_sem=h_recv.at[c],
            device_id={"ctx": right},
            device_id_type=MESH,
        )

    @pl.loop(0, chunks)
    def _(c):
        halo(c).start()

    for i in (4, 5, 6):
        loads[i].wait()

    rate_t = rate_r[...]
    scale_t = resid_r[...] * jnp.sqrt(one_minus_exp_neg(2.0 * rate_t))
    scale_r[...] = scale_t
    lane1 = iota((1, LANES), 1)
    flip = (iota((TAPS, LANES), 0) == ((LANES - iota((TAPS, LANES), 1)) & (LANES - 1))).astype(BF16)
    tap_row[...] = jnp.dot(taps_r[...], flip, preferred_element_type=F32)

    rate = rate_t.T
    scale = scale_t.T
    lag = ((STEP - iota((groups, LANES), 1) % STEP) % STEP).astype(F32)
    acc = jnp.zeros((groups, LANES), F32)
    for p in range(poles):
        acc = acc + scale[:, p : p + 1] * jnp.exp(-rate[:, p : p + 1] * lag)
    lag_row[...] = acc

    x_i = iota((8, LANES), 1)
    t_i = iota((8, LANES), 0)
    lane_p = iota((poles, LANES), 1)
    pole_p = iota((poles, LANES), 0)
    seg, off = lane1 // STEP, lane1 % STEP

    def skewed(row):
        first = pltpu.roll(jnp.broadcast_to(row, (8, LANES)), 0, 1, stride=1, stride_axis=0)
        return [first] + [pltpu.roll(first, 8 * m, 1) for m in range(1, STEP // 8)]

    def tables(j):
        lanes = block(j)
        for g in range(gb):
            at = pl.ds(pl.multiple_of((j * gb + g) * STEP, STEP), STEP)
            parts = skewed(tap_row[pl.ds(j * gb + g, 1), :])
            far = [jnp.where(x_i > t_i + 8 * m, part, 0.0) for m, part in enumerate(parts)]
            own = [jnp.where(x_i > t_i + 8 * m, 0.0, part) for m, part in enumerate(parts)]
            t_mr[at, 0:LANES] = jnp.concatenate(far, axis=0).astype(BF16)
            t_mr[at, LANES:] = jnp.concatenate(own, axis=0).astype(BF16)
        for h in range(gb // QUAD):
            base = pl.multiple_of(j * 2 * (STEP + poles), 16)
            quad = (j * gb) + h * QUAD
            row = jnp.zeros((1, LANES), F32)
            for r in range(QUAD):
                here = ((off == 0) & (seg == r)) | ((off > 0) & (seg == (r - 1) % QUAD))
                row = jnp.where(here, lag_row[pl.ds(quad + r, 1), :], row)
            parts = skewed(row)
            own = [jnp.where((x_i % STEP) > t_i + 8 * m, 0.0, part) for m, part in enumerate(parts)]
            t_li[pl.ds(base + h * STEP, STEP), :] = jnp.concatenate(own, axis=0).astype(BF16)
            r_q = jnp.take_along_axis(rate_r[...], quad + lane_p // STEP, axis=1)
            w = jnp.exp(-r_q * (STEP - 1 - lane_p % STEP).astype(F32))
            t_li[pl.ds(base + 2 * STEP + h * poles, poles), :] = w.astype(BF16)
        index = j * gb + lane_p // width
        r_c = jnp.take_along_axis(rate_r[...], index, axis=1)
        s_c = jnp.take_along_axis(scale_r[...], index, axis=1)
        dec_step[:, lanes] = jnp.exp(-float(STEP) * r_c)
        dec_all[:, lanes] = jnp.exp(-float(rows) * r_c)
        diag = pole_p == lane_p % poles
        r_l = jnp.sum(jnp.where(diag, r_c, 0.0), axis=0, keepdims=True)
        s_l = jnp.sum(jnp.where(diag, s_c, 0.0), axis=0, keepdims=True)
        carry_w[:, lanes] = (s_l * jnp.exp(-r_l * (iota((STEP, LANES), 0) + 1).astype(F32))).astype(BF16)

    for k in range(2):
        widen(k)

        @pl.loop(k * blocks // 2, (k + 1) * blocks // 2)
        def _(j):
            tables(j)

    widen(2)
    widen(3)

    loads[2].wait()
    loads[3].wait()
    u_ext[TAPS:rows, :] = kb[: rows - TAPS, :] * vb[: rows - TAPS, :]
    loads[7].wait()
    loads[8].wait()

    group_w = (iota((STEP, rows // STEP * LANES), 1) % LANES) // width
    left_t = (iota((STEP, rows // STEP * LANES), 1) % LANES) < LANES // 2
    left_p = (iota((poles, rows // STEP * LANES), 1) % LANES) < LANES // 2
    quad_g = (iota((STEP, LANES), 1) // width) % QUAD
    pole_g = iota((poles, LANES), 1) // width

    def wait_pieces(sem, count):
        pltpu.make_async_copy(e_out.at[pl.ds(0, count)], s_in.at[pl.ds(0, count)], sem).wait()

    def piece(o):
        return pl.ds(pl.multiple_of(8 * lax.rem(o, 2), 8), 8), block(o // 2)

    def state_copy(o, frm):
        return pltpu.make_async_remote_copy(
            src_ref=s_loc.at[o], dst_ref=s_in.at[frm], send_sem=s_send, recv_sem=s_recv,
            device_id={"ctx": o}, device_id_type=MESH,
        )

    def short(j):
        lanes = block(j)
        at = pl.ds(pl.multiple_of(j * gb * STEP, gb * STEP), gb * STEP)
        rhs = jnp.concatenate([u_ext[a * STEP : a * STEP + window, lanes] for a in range(steps)], axis=1)
        res = jnp.dot(t_mr[at, 0:window], rhs, preferred_element_type=F32)
        conv = res[0:STEP]
        for g in range(1, gb):
            conv = jnp.where(group_w == g, res[g * STEP : (g + 1) * STEP], conv)
        diag = []
        for a in range(steps):
            part = pl.ds(a * STEP, STEP)
            out = (qb[part, lanes].astype(F32) * conv[:, a * LANES : (a + 1) * LANES]).astype(BF16)
            mr_h[part, lanes] = out
            u_li = klb[part, lanes] * out
            diag.append(jnp.concatenate([jnp.where(quad_g == r, u_li, jnp.zeros_like(u_li)) for r in range(QUAD)], axis=0))
        return jnp.concatenate(diag, axis=1)

    def long(j, diag):
        lanes = block(j)
        li_at = pl.ds(pl.multiple_of(j * 2 * (STEP + poles), 16), 2 * (STEP + poles))
        step_dec = dec_step[:, lanes]
        res = jnp.dot(t_li[li_at, :], diag, preferred_element_type=F32)
        own = jnp.where(left_t, res[0:STEP], res[STEP : 2 * STEP])
        ends = jnp.where(left_p, res[2 * STEP : 2 * STEP + poles], res[2 * STEP + poles :])
        state = None
        for a in range(steps):
            cut = slice(a * LANES, (a + 1) * LANES)
            near[pl.ds(a * STEP, STEP), lanes] = own[:, cut]
            if a == 0:
                state = ends[:, cut]
            else:
                s_part[a, :, lanes] = state
                state = state * step_dec + ends[:, cut]
        for h in range(2):
            s_loc[2 * j + h] = state[8 * h : 8 * h + 8].astype(BF16)

    def hand_out(j):
        for h in range(2):
            o = 2 * j + h

            @pl.when(o != me)
            def _():
                state_copy(o, me).start()

            @pl.when(o == me)
            def _():
                s_in[me] = s_loc[o]

    def enter_copy(owner, to):
        return pltpu.make_async_remote_copy(
            src_ref=e_out.at[to], dst_ref=e_loc.at[owner], send_sem=e_send, recv_sem=e_recv.at[owner // per_chunk],
            device_id={"ctx": to}, device_id_type=MESH,
        )

    def scan_owned():
        wait_pieces(s_recv, n - 1)
        my_a, my_b = piece(me)
        my_dec = dec_all[my_a, my_b]
        carried = jnp.zeros((8, LANES), F32)
        for b in range(n):
            e_out[b] = carried.astype(BF16)
            if b + 1 < n:
                carried = carried * my_dec + s_in[b].astype(F32)

        @pl.loop(1, n)
        def _(i):
            enter_copy(me, lax.rem(me + i, n)).start()

        e_loc[me] = e_out[me]

    @pl.loop(0, chunks)
    def _(c):
        halo(c).wait_recv()

        @pl.when(me == 0)
        def _():
            lanes = pl.ds(pl.multiple_of(c * cw, cw), cw)
            u_ext[0:TAPS, lanes] = jnp.zeros((TAPS, cw), BF16)

        js = [c * CHUNK_BLOCKS + i for i in range(CHUNK_BLOCKS)]
        diags = [short(j) for j in js]
        for j, diag in zip(js, diags):
            long(j, diag)
        for j in js:
            hand_out(j)

        @pl.when(c == scan_at)
        def _():
            scan_owned()

    @pl.when(scan_at >= chunks)
    def _():
        scan_owned()

    loads[9].wait()


    def finish(j):
        lanes = block(j)
        e = jnp.concatenate([e_loc[2 * j], e_loc[2 * j + 1]], axis=0).astype(F32)
        step_dec = dec_step[:, lanes]
        diag = []
        for a in range(steps):
            state = (s_part[a, :, lanes] + e if a else e).astype(BF16)
            diag.append(jnp.concatenate([jnp.where(pole_g == g, state, jnp.zeros_like(state)) for g in range(gb)], axis=0))
            e = e * step_dec
        far = jnp.dot(carry_w[:, lanes], jnp.concatenate(diag, axis=1), preferred_element_type=F32)
        for a in range(steps):
            part = pl.ds(a * STEP, STEP)
            conv = near[part, lanes] + far[:, a * LANES : (a + 1) * LANES]
            li_h[part, lanes] = (qlb[part, lanes].astype(F32) * conv).astype(BF16)

    @pl.loop(0, chunks)
    def _(c):
        @pl.when(c == me // per_chunk)
        def _():
            wait_pieces(e_recv.at[c], per_chunk - 1)

        @pl.when(c != me // per_chunk)
        def _():
            wait_pieces(e_recv.at[c], per_chunk)

        for i in range(CHUNK_BLOCKS):
            finish(c * CHUNK_BLOCKS + i)

    pltpu.make_async_copy(u_ext.at[pl.ds(rows, TAPS)], u_ext.at[pl.ds(0, TAPS)], h_send).wait()
    wait_pieces(s_send, n - 1)
    wait_pieces(e_send, n - 1)


def store(a_ref, b_ref, a_h, b_h, sem):
    size = a_ref.shape[0] // STORES
    copies = []
    for i in range(STORES):
        at = pl.ds(i * size, size)
        copies.append(pltpu.make_async_copy(a_ref.at[at], a_h.at[at], sem.at[2 * i]))
        copies.append(pltpu.make_async_copy(b_ref.at[at], b_h.at[at], sem.at[2 * i + 1]))
    for copy in copies:
        copy.start()
    for copy in copies:
        copy.wait()


def body(n, q, k, v, ql, kl, taps, rate, resid):
    rows, channels = q.shape
    groups, poles = rate.shape
    width = channels // groups
    blocks = channels // LANES
    chunks = blocks // CHUNK_BLOCKS
    assert n == 32 and taps.shape[1] == TAPS and 2 * blocks == n and width == poles == 16
    dma = pltpu.SemaphoreType.DMA
    vm = pltpu.VMEM
    hbm = pl.BlockSpec(memory_space=pltpu.HBM)
    small = pl.BlockSpec(memory_space=pltpu.VMEM)
    full = vm((rows, channels), BF16)
    out = jax.ShapeDtypeStruct((rows, channels), BF16)
    decays = vm((poles, channels), F32)
    states = vm((n, 8, LANES), BF16)
    results = pl.pallas_call(
        functools.partial(kernel, n, width, poles),
        out_shape=(out, out),
        in_specs=[hbm] * 8,
        out_specs=(small, small),
        scratch_shapes=[
            full, full, full, full, full,
            vm(taps.shape, BF16), vm((poles, groups), F32), vm((poles, groups), F32),
            vm((TAPS + rows, channels), BF16),
            vm((groups * STEP, 2 * LANES), BF16),
            vm((blocks * 2 * (STEP + poles), LANES), BF16),
            vm((STEP, groups * poles), BF16),
            vm((rows, channels), F32),
            vm((rows // STEP, poles, channels), F32),
            states, states, states, states,
            vm((groups, LANES), F32), vm((groups, LANES), F32), vm((poles, groups), F32), decays, decays,
            pltpu.SemaphoreType.REGULAR((4,)), dma((10,)), dma(()), dma((chunks,)), dma(()), dma(()), dma(()), dma((chunks,)),
        ],
        compiler_params=pltpu.CompilerParams(collective_id=0, has_side_effects=True, vmem_limit_bytes=28 << 20),
        cost_estimate=pl.CostEstimate(flops=4 * 10**9, bytes_accessed=8 << 20, transcendentals=0),
    )(*[pltpu.with_memory_space_constraint(x, pltpu.HBM) for x in (q, k, v, ql, kl, taps, rate.T, resid.T)])
    return pl.pallas_call(
        store,
        out_shape=(out, out),
        in_specs=[small] * 2,
        out_specs=(hbm, hbm),
        scratch_shapes=[dma((2 * STORES,))],
        compiler_params=pltpu.CompilerParams(vmem_limit_bytes=4 << 20),
        cost_estimate=pl.CostEstimate(flops=0, bytes_accessed=4 << 20, transcendentals=0),
    )(*results)


def solution(mesh):
    rep_ctx = ("rep", "ctx")
    big = P(rep_ctx, "tp")
    return jax.shard_map(
        functools.partial(body, mesh.shape["ctx"]),
        mesh=mesh,
        in_specs=(big,) * 5 + (P("tp", None),) * 3,
        out_specs=(big, big),
        check_vma=False,
    )
```

```python
import functools

import jax
import jax.numpy as jnp
from jax import lax
from jax.experimental import pallas as pl
from jax.experimental.pallas import tpu as pltpu
from jax.sharding import PartitionSpec as P

MESH = pl.DeviceIdType.MESH
F32 = jnp.float32
BF16 = jnp.bfloat16
LANES = 128
TAPS = 128
STEP = 32
QUAD = LANES // STEP
STORES = 4
CHUNK_BLOCKS = 2


def one_minus_exp_neg(x):
    s = x * (1.0 - x * (1 / 2) * (1.0 - x * (1 / 3) * (1.0 - x * (1 / 4) * (1.0 - x * (1 / 5) * (1.0 - x * (1 / 6) * (1.0 - x * (1 / 7)))))))
    return jnp.where(x < 0.25, s, 1.0 - jnp.exp(-x))


def iota(shape, dim):
    return lax.broadcasted_iota(jnp.int32, shape, dim)


def kernel(
    n, width, poles,
    q_h, k_h, v_h, ql_h, kl_h, taps_h, rate_h, resid_h,
    mr_h, li_h,
    kb, vb, qb, qlb, klb, taps_r, rate_r, resid_r, u_ext, t_mr, t_li, carry_w, near, s_part,
    s_loc, s_in, e_out, e_loc, tap_row, lag_row, scale_r, rate_l, scale_l, dec_step, dec_all,
    known, in_sem, h_send, h_recv, s_send, s_recv, e_send, e_recv,
):
    me = lax.axis_index("ctx")
    right = lax.rem(me + 1, n)
    rows, channels = kb.shape
    groups = channels // width
    blocks = channels // LANES
    gb = LANES // width
    steps = rows // STEP
    window = TAPS + STEP
    chunks = blocks // CHUNK_BLOCKS
    cw = CHUNK_BLOCKS * LANES
    per_chunk = 2 * CHUNK_BLOCKS

    barrier = pltpu.get_barrier_semaphore()

    def greet(sem, far):
        for i in (far, n - far):
            pl.semaphore_signal(sem, inc=1, device_id={"ctx": lax.rem(me + i, n)}, device_id_type=MESH)

    greet(barrier, 1)

    def inp(src, dst, i):
        return pltpu.make_async_copy(src, dst, in_sem.at[i])

    tail, head = pl.ds(rows - TAPS, TAPS), pl.ds(0, rows - TAPS)
    side = [pl.ds(i * channels // 2, channels // 2) for i in range(2)]
    loads = [
        inp(k_h.at[tail, side[0]], kb.at[tail, side[0]], 0),
        inp(v_h.at[tail, side[0]], vb.at[tail, side[0]], 1),
        inp(k_h.at[tail, side[1]], kb.at[tail, side[1]], 10),
        inp(v_h.at[tail, side[1]], vb.at[tail, side[1]], 11),
        inp(k_h.at[head], kb.at[head], 2),
        inp(v_h.at[head], vb.at[head], 3),
        inp(taps_h, taps_r, 7),
        inp(rate_h, rate_r, 8),
        inp(resid_h, resid_r, 9),
        inp(q_h, qb, 4),
        inp(kl_h, klb, 5),
        inp(ql_h, qlb, 6),
    ]
    for copy in loads:
        copy.start()


    def widen(k):
        pl.semaphore_wait(known.at[k], 2)
        if k < 3:
            greet(known.at[k + 1], 2 ** (k + 1))

    def block(j):
        return pl.ds(pl.multiple_of(j * LANES, LANES), LANES)

    def halo(c):
        lanes = pl.ds(pl.multiple_of(c * cw, cw), cw)
        return pltpu.make_async_remote_copy(
            src_ref=u_ext.at[pl.ds(rows, TAPS), lanes],
            dst_ref=u_ext.at[pl.ds(0, TAPS), lanes],
            send_sem=h_send,
            recv_sem=h_recv.at[c],
            device_id={"ctx": right},
            device_id_type=MESH,
        )

    for i in range(2):
        loads[2 * i].wait()
        loads[2 * i + 1].wait()
        u_ext[rows:, side[i]] = kb[rows - TAPS :, side[i]] * vb[rows - TAPS :, side[i]]
        if i == 0:
            pl.semaphore_wait(barrier, 2)

        @pl.loop(i * chunks // 2, (i + 1) * chunks // 2)
        def _(c):
            halo(c).start()

    greet(known.at[0], 1)

    for i in (6, 7, 8):
        loads[i].wait()

    rate_t = rate_r[...]
    scale_t = resid_r[...] * jnp.sqrt(one_minus_exp_neg(2.0 * rate_t))
    scale_r[...] = scale_t
    lane1 = iota((1, LANES), 1)
    flip = (iota((TAPS, LANES), 0) == ((LANES - iota((TAPS, LANES), 1)) & (LANES - 1))).astype(BF16)
    tap_row[...] = jnp.dot(taps_r[...], flip, preferred_element_type=F32)

    rate = rate_t.T
    scale = scale_t.T
    lag = ((STEP - iota((groups, LANES), 1) % STEP) % STEP).astype(F32)
    acc = jnp.zeros((groups, LANES), F32)
    for p in range(poles):
        acc = acc + scale[:, p : p + 1] * jnp.exp(-rate[:, p : p + 1] * lag)
    lag_row[...] = acc

    x_i = iota((8, LANES), 1)
    t_i = iota((8, LANES), 0)
    lane_p = iota((poles, LANES), 1)
    pole_p = iota((poles, LANES), 0)
    seg, off = lane1 // STEP, lane1 % STEP

    def skewed(row):
        first = pltpu.roll(jnp.broadcast_to(row, (8, LANES)), 0, 1, stride=1, stride_axis=0)
        return [first] + [pltpu.roll(first, 8 * m, 1) for m in range(1, STEP // 8)]

    def tables(j):
        lanes = block(j)
        for g in range(gb):
            at = pl.ds(pl.multiple_of((j * gb + g) * STEP, STEP), STEP)
            parts = skewed(tap_row[pl.ds(j * gb + g, 1), :])
            far = [jnp.where(x_i > t_i + 8 * m, part, 0.0) for m, part in enumerate(parts)]
            own = [jnp.where(x_i > t_i + 8 * m, 0.0, part) for m, part in enumerate(parts)]
            t_mr[at, 0:LANES] = jnp.concatenate(far, axis=0).astype(BF16)
            t_mr[at, LANES:] = jnp.concatenate(own, axis=0).astype(BF16)
        for h in range(gb // QUAD):
            base = pl.multiple_of(j * 2 * (STEP + poles), 16)
            quad = (j * gb) + h * QUAD
            row = jnp.zeros((1, LANES), F32)
            for r in range(QUAD):
                here = ((off == 0) & (seg == r)) | ((off > 0) & (seg == (r - 1) % QUAD))
                row = jnp.where(here, lag_row[pl.ds(quad + r, 1), :], row)
            parts = skewed(row)
            own = [jnp.where((x_i % STEP) > t_i + 8 * m, 0.0, part) for m, part in enumerate(parts)]
            t_li[pl.ds(base + h * STEP, STEP), :] = jnp.concatenate(own, axis=0).astype(BF16)
            r_q = jnp.take_along_axis(rate_r[...], quad + lane_p // STEP, axis=1)
            w = jnp.exp(-r_q * (STEP - 1 - lane_p % STEP).astype(F32))
            t_li[pl.ds(base + 2 * STEP + h * poles, poles), :] = w.astype(BF16)
        index = j * gb + lane_p // width
        r_c = jnp.take_along_axis(rate_r[...], index, axis=1)
        s_c = jnp.take_along_axis(scale_r[...], index, axis=1)
        dec_step[:, lanes] = jnp.exp(-float(STEP) * r_c)
        dec_all[:, lanes] = jnp.exp(-float(rows) * r_c)
        diag = pole_p == lane_p % poles
        r_l = jnp.sum(jnp.where(diag, r_c, 0.0), axis=0, keepdims=True)
        s_l = jnp.sum(jnp.where(diag, s_c, 0.0), axis=0, keepdims=True)
        rate_l[:, lanes] = r_l
        scale_l[:, lanes] = s_l
        carry_w[0:STEP, lanes] = (s_l * jnp.exp(-r_l * (iota((STEP, LANES), 0) + 1).astype(F32))).astype(BF16)

    for k in range(2):
        widen(k)

        @pl.loop(k * blocks // 2, (k + 1) * blocks // 2)
        def _(j):
            tables(j)


    loads[4].wait()
    loads[5].wait()
    u_ext[TAPS:rows, :] = kb[: rows - TAPS, :] * vb[: rows - TAPS, :]
    loads[9].wait()
    loads[10].wait()

    group_w = (iota((STEP, rows // STEP * LANES), 1) % LANES) // width
    left_t = (iota((STEP, rows // STEP * LANES), 1) % LANES) < LANES // 2
    left_p = (iota((poles, rows // STEP * LANES), 1) % LANES) < LANES // 2
    quad_g = (iota((STEP, LANES), 1) // width) % QUAD
    pole_g = iota((poles, LANES), 1) // width

    def wait_pieces(sem, count):
        pltpu.make_async_copy(e_out.at[pl.ds(0, count)], s_in.at[pl.ds(0, count)], sem).wait()

    def piece(o):
        return pl.ds(pl.multiple_of(8 * lax.rem(o, 2), 8), 8), block(o // 2)

    def state_copy(o, frm):
        return pltpu.make_async_remote_copy(
            src_ref=s_loc.at[o], dst_ref=s_in.at[frm], send_sem=s_send, recv_sem=s_recv,
            device_id={"ctx": o}, device_id_type=MESH,
        )

    def short(j):
        lanes = block(j)
        at = pl.ds(pl.multiple_of(j * gb * STEP, gb * STEP), gb * STEP)
        rhs = jnp.concatenate([u_ext[a * STEP : a * STEP + window, lanes] for a in range(steps)], axis=1)
        res = jnp.dot(t_mr[at, 0:window], rhs, preferred_element_type=F32)
        conv = res[0:STEP]
        for g in range(1, gb):
            conv = jnp.where(group_w == g, res[g * STEP : (g + 1) * STEP], conv)
        diag = []
        for a in range(steps):
            part = pl.ds(a * STEP, STEP)
            out = (qb[part, lanes].astype(F32) * conv[:, a * LANES : (a + 1) * LANES]).astype(BF16)
            mr_h[part, lanes] = out
            u_li = klb[part, lanes] * out
            diag.append(jnp.concatenate([jnp.where(quad_g == r, u_li, jnp.zeros_like(u_li)) for r in range(QUAD)], axis=0))
        return jnp.concatenate(diag, axis=1)

    def long(j, diag):
        lanes = block(j)
        li_at = pl.ds(pl.multiple_of(j * 2 * (STEP + poles), 16), 2 * (STEP + poles))
        step_dec = dec_step[:, lanes]
        res = jnp.dot(t_li[li_at, :], diag, preferred_element_type=F32)
        own = jnp.where(left_t, res[0:STEP], res[STEP : 2 * STEP])
        ends = jnp.where(left_p, res[2 * STEP : 2 * STEP + poles], res[2 * STEP + poles :])
        state = None
        for a in range(steps):
            cut = slice(a * LANES, (a + 1) * LANES)
            near[pl.ds(a * STEP, STEP), lanes] = own[:, cut]
            if a == 0:
                state = ends[:, cut]
            else:
                s_part[a, :, lanes] = state
                state = state * step_dec + ends[:, cut]
        for h in range(2):
            s_loc[2 * j + h] = state[8 * h : 8 * h + 8].astype(BF16)

    def hand_out(j):
        for h in range(2):
            o = 2 * j + h

            @pl.when(o != me)
            def _():
                state_copy(o, me).start()

            @pl.when(o == me)
            def _():
                s_in[me] = s_loc[o]

    def enter_copy(owner, to):
        return pltpu.make_async_remote_copy(
            src_ref=e_out.at[to], dst_ref=e_loc.at[owner], send_sem=e_send, recv_sem=e_recv.at[owner // per_chunk],
            device_id={"ctx": to}, device_id_type=MESH,
        )

    def scan_owned():
        wait_pieces(s_recv, n - 1)
        my_a, my_b = piece(me)
        my_dec = dec_all[my_a, my_b]
        carried = jnp.zeros((8, LANES), F32)
        for b in range(n):
            e_out[b] = carried.astype(BF16)
            if b + 1 < n:
                carried = carried * my_dec + s_in[b].astype(F32)

        @pl.loop(1, n)
        def _(i):
            enter_copy(me, lax.rem(me + i, n)).start()

        e_loc[me] = e_out[me]

    @pl.loop(0, chunks)
    def _(c):
        halo(c).wait_recv()

        @pl.when(me == 0)
        def _():
            lanes = pl.ds(pl.multiple_of(c * cw, cw), cw)
            u_ext[0:TAPS, lanes] = jnp.zeros((TAPS, cw), BF16)

        js = [c * CHUNK_BLOCKS + i for i in range(CHUNK_BLOCKS)]
        diags = [short(j) for j in js]
        for j, diag in zip(js, diags):
            long(j, diag)
        @pl.when(c == 0)
        def _():
            widen(2)

        @pl.when(c == 1)
        def _():
            widen(3)
            for i in range(CHUNK_BLOCKS):
                hand_out(i)

        @pl.when(c > 0)
        def _():
            for j in js:
                hand_out(j)

    def spread_out(state):
        return jnp.concatenate([jnp.where(pole_g == g, state, jnp.zeros_like(state)) for g in range(gb)], axis=0)

    def from_own_states(j):
        lanes = block(j)
        diag = [spread_out(s_part[a, :, lanes].astype(BF16)) for a in range(1, steps)]
        add = jnp.dot(carry_w[0:STEP, lanes], jnp.concatenate(diag, axis=1), preferred_element_type=F32)
        for a in range(1, steps):
            near[pl.ds(a * STEP, STEP), lanes] += add[:, (a - 1) * LANES : a * LANES]
        pos = iota((rows - STEP, LANES), 0) + (STEP + 1)
        carry_w[STEP:, lanes] = (scale_l[:, lanes] * jnp.exp(-rate_l[:, lanes] * pos.astype(F32))).astype(BF16)

    @pl.loop(0, chunks)
    def _(c):
        for i in range(CHUNK_BLOCKS):
            from_own_states(c * CHUNK_BLOCKS + i)

    scan_owned()

    loads[11].wait()


    def finish(c):
        lanes = pl.ds(pl.multiple_of(c * cw, cw), cw)
        zero = jnp.zeros((LANES, LANES), BF16)
        a, b = [spread_out(jnp.concatenate([e_loc[2 * j], e_loc[2 * j + 1]], axis=0)) for j in (2 * c, 2 * c + 1)]
        diag = jnp.concatenate([jnp.concatenate([a, zero], axis=0), jnp.concatenate([zero, b], axis=0)], axis=1)
        for part in [pl.ds(i, 128) for i in range(0, rows, 128)]:
            far = jnp.dot(carry_w[part, lanes], diag, preferred_element_type=F32)
            li_h[part, lanes] = (qlb[part, lanes].astype(F32) * (near[part, lanes] + far)).astype(BF16)

    @pl.loop(0, chunks)
    def _(c):
        @pl.when(c == me // per_chunk)
        def _():
            wait_pieces(e_recv.at[c], per_chunk - 1)

        @pl.when(c != me // per_chunk)
        def _():
            wait_pieces(e_recv.at[c], per_chunk)

        finish(c)

    pltpu.make_async_copy(u_ext.at[pl.ds(rows, TAPS)], u_ext.at[pl.ds(0, TAPS)], h_send).wait()
    wait_pieces(s_send, n - 1)
    wait_pieces(e_send, n - 1)


def store(a_ref, b_ref, a_h, b_h, sem):
    size = a_ref.shape[0] // STORES
    copies = []
    for i in range(STORES):
        at = pl.ds(i * size, size)
        copies.append(pltpu.make_async_copy(a_ref.at[at], a_h.at[at], sem.at[2 * i]))
        copies.append(pltpu.make_async_copy(b_ref.at[at], b_h.at[at], sem.at[2 * i + 1]))
    for copy in copies:
        copy.start()
    for copy in copies:
        copy.wait()


def body(n, q, k, v, ql, kl, taps, rate, resid):
    rows, channels = q.shape
    groups, poles = rate.shape
    width = channels // groups
    blocks = channels // LANES
    chunks = blocks // CHUNK_BLOCKS
    assert n == 32 and taps.shape[1] == TAPS and 2 * blocks == n and width == poles == 16
    dma = pltpu.SemaphoreType.DMA
    vm = pltpu.VMEM
    hbm = pl.BlockSpec(memory_space=pltpu.HBM)
    small = pl.BlockSpec(memory_space=pltpu.VMEM)
    full = vm((rows, channels), BF16)
    out = jax.ShapeDtypeStruct((rows, channels), BF16)
    decays = vm((poles, channels), F32)
    states = vm((n, 8, LANES), BF16)
    results = pl.pallas_call(
        functools.partial(kernel, n, width, poles),
        out_shape=(out, out),
        in_specs=[hbm] * 8,
        out_specs=(small, small),
        scratch_shapes=[
            full, full, full, full, full,
            vm(taps.shape, BF16), vm((poles, groups), F32), vm((poles, groups), F32),
            vm((TAPS + rows, channels), BF16),
            vm((groups * STEP, 2 * LANES), BF16),
            vm((blocks * 2 * (STEP + poles), LANES), BF16),
            vm((rows, groups * poles), BF16),
            vm((rows, channels), F32),
            vm((rows // STEP, poles, channels), F32),
            states, states, states, states,
            vm((groups, LANES), F32), vm((groups, LANES), F32), vm((poles, groups), F32), vm((1, channels), F32), vm((1, channels), F32), decays, decays,
            pltpu.SemaphoreType.REGULAR((4,)), dma((12,)), dma(()), dma((chunks,)), dma(()), dma(()), dma(()), dma((chunks,)),
        ],
        compiler_params=pltpu.CompilerParams(collective_id=0, has_side_effects=True, vmem_limit_bytes=28 << 20),
        cost_estimate=pl.CostEstimate(flops=4 * 10**9, bytes_accessed=8 << 20, transcendentals=0),
    )(*[pltpu.with_memory_space_constraint(x, pltpu.HBM) for x in (q, k, v, ql, kl, taps, rate.T, resid.T)])
    return pl.pallas_call(
        store,
        out_shape=(out, out),
        in_specs=[small] * 2,
        out_specs=(hbm, hbm),
        scratch_shapes=[dma((2 * STORES,))],
        compiler_params=pltpu.CompilerParams(vmem_limit_bytes=4 << 20),
        cost_estimate=pl.CostEstimate(flops=0, bytes_accessed=4 << 20, transcendentals=0),
    )(*results)


def solution(mesh):
    rep_ctx = ("rep", "ctx")
    big = P(rep_ctx, "tp")
    return jax.shard_map(
        functools.partial(body, mesh.shape["ctx"]),
        mesh=mesh,
        in_specs=(big,) * 5 + (P("tp", None),) * 3,
        out_specs=(big, big),
        check_vma=False,
    )
```

```python
import functools

import jax
import jax.numpy as jnp
from jax import lax
from jax.experimental import pallas as pl
from jax.experimental.pallas import tpu as pltpu
from jax.sharding import PartitionSpec as P

MESH = pl.DeviceIdType.MESH
F32 = jnp.float32
BF16 = jnp.bfloat16
LANES = 128
TAPS = 128
STEP = 32
QUAD = LANES // STEP
STORES = 4
CHUNK_BLOCKS = 2


def one_minus_exp_neg(x):
    s = x * (1.0 - x * (1 / 2) * (1.0 - x * (1 / 3) * (1.0 - x * (1 / 4) * (1.0 - x * (1 / 5) * (1.0 - x * (1 / 6) * (1.0 - x * (1 / 7)))))))
    return jnp.where(x < 0.25, s, 1.0 - jnp.exp(-x))


def iota(shape, dim):
    return lax.broadcasted_iota(jnp.int32, shape, dim)


def kernel(
    n, width, poles,
    q_h, k_h, v_h, ql_h, kl_h, taps_h, rate_h, resid_h,
    mr_h, li_h,
    kb, vb, qb, qlb, klb, taps_r, rate_r, resid_r, u_ext, t_mr, t_li, carry_w, near, s_part,
    s_loc, s_in, e_out, e_loc, tap_row, lag_row, scale_r, rate_l, scale_l, dec_step, dec_all,
    known, in_sem, h_send, h_recv, s_send, s_recv, e_send, e_recv,
):
    me = lax.axis_index("ctx")
    right = lax.rem(me + 1, n)
    rows, channels = kb.shape
    groups = channels // width
    blocks = channels // LANES
    gb = LANES // width
    steps = rows // STEP
    window = TAPS + STEP
    chunks = blocks // CHUNK_BLOCKS
    cw = CHUNK_BLOCKS * LANES
    per_chunk = 2 * CHUNK_BLOCKS

    barrier = pltpu.get_barrier_semaphore()

    def greet(sem, far):
        for i in (far, n - far):
            pl.semaphore_signal(sem, inc=1, device_id={"ctx": lax.rem(me + i, n)}, device_id_type=MESH)

    greet(barrier, 1)

    def inp(src, dst, i):
        return pltpu.make_async_copy(src, dst, in_sem.at[i])

    tail, head = pl.ds(rows - TAPS, TAPS), pl.ds(0, rows - TAPS)
    side = [pl.ds(i * channels // 2, channels // 2) for i in range(2)]
    loads = [
        inp(k_h.at[tail, side[0]], kb.at[tail, side[0]], 0),
        inp(v_h.at[tail, side[0]], vb.at[tail, side[0]], 1),
        inp(k_h.at[tail, side[1]], kb.at[tail, side[1]], 10),
        inp(v_h.at[tail, side[1]], vb.at[tail, side[1]], 11),
        inp(k_h.at[head], kb.at[head], 2),
        inp(v_h.at[head], vb.at[head], 3),
        inp(taps_h, taps_r, 7),
        inp(rate_h, rate_r, 8),
        inp(resid_h, resid_r, 9),
        inp(q_h, qb, 4),
        inp(kl_h, klb, 5),
        inp(ql_h, qlb, 6),
    ]
    for copy in loads:
        copy.start()


    def widen(k):
        pl.semaphore_wait(known.at[k], 2)
        if k < 3:
            greet(known.at[k + 1], 2 ** (k + 1))

    def block(j):
        return pl.ds(pl.multiple_of(j * LANES, LANES), LANES)

    def halo(c):
        lanes = pl.ds(pl.multiple_of(c * cw, cw), cw)
        return pltpu.make_async_remote_copy(
            src_ref=u_ext.at[pl.ds(rows, TAPS), lanes],
            dst_ref=u_ext.at[pl.ds(0, TAPS), lanes],
            send_sem=h_send,
            recv_sem=h_recv.at[c],
            device_id={"ctx": right},
            device_id_type=MESH,
        )

    for i in range(2):
        loads[2 * i].wait()
        loads[2 * i + 1].wait()
        u_ext[rows:, side[i]] = kb[rows - TAPS :, side[i]] * vb[rows - TAPS :, side[i]]
        if i == 0:
            pl.semaphore_wait(barrier, 2)

        @pl.loop(i * chunks // 2, (i + 1) * chunks // 2)
        def _(c):
            halo(c).start()

    greet(known.at[0], 1)

    for i in (6, 7, 8):
        loads[i].wait()

    rate_t = rate_r[...]
    scale_t = resid_r[...] * jnp.sqrt(one_minus_exp_neg(2.0 * rate_t))
    scale_r[...] = scale_t
    lane1 = iota((1, LANES), 1)
    flip = (iota((TAPS, LANES), 0) == ((LANES - iota((TAPS, LANES), 1)) & (LANES - 1))).astype(BF16)
    tap_row[...] = jnp.dot(taps_r[...], flip, preferred_element_type=F32)

    rate = rate_t.T
    scale = scale_t.T
    lag = ((STEP - iota((groups, LANES), 1) % STEP) % STEP).astype(F32)
    acc = jnp.zeros((groups, LANES), F32)
    for p in range(poles):
        acc = acc + scale[:, p : p + 1] * jnp.exp(-rate[:, p : p + 1] * lag)
    lag_row[...] = acc

    x_i = iota((8, LANES), 1)
    t_i = iota((8, LANES), 0)
    lane_p = iota((poles, LANES), 1)
    pole_p = iota((poles, LANES), 0)
    seg, off = lane1 // STEP, lane1 % STEP

    def skewed(row):
        first = pltpu.roll(jnp.broadcast_to(row, (8, LANES)), 0, 1, stride=1, stride_axis=0)
        return [first] + [pltpu.roll(first, 8 * m, 1) for m in range(1, STEP // 8)]

    def tables(j):
        lanes = block(j)
        for g in range(gb):
            at = pl.ds(pl.multiple_of((j * gb + g) * STEP, STEP), STEP)
            parts = skewed(tap_row[pl.ds(j * gb + g, 1), :])
            far = [jnp.where(x_i > t_i + 8 * m, part, 0.0) for m, part in enumerate(parts)]
            own = [jnp.where(x_i > t_i + 8 * m, 0.0, part) for m, part in enumerate(parts)]
            t_mr[at, 0:LANES] = jnp.concatenate(far, axis=0).astype(BF16)
            t_mr[at, LANES:] = jnp.concatenate(own, axis=0).astype(BF16)
        for h in range(gb // QUAD):
            base = pl.multiple_of(j * 2 * (STEP + poles), 16)
            quad = (j * gb) + h * QUAD
            row = jnp.zeros((1, LANES), F32)
            for r in range(QUAD):
                here = ((off == 0) & (seg == r)) | ((off > 0) & (seg == (r - 1) % QUAD))
                row = jnp.where(here, lag_row[pl.ds(quad + r, 1), :], row)
            parts = skewed(row)
            own = [jnp.where((x_i % STEP) > t_i + 8 * m, 0.0, part) for m, part in enumerate(parts)]
            t_li[pl.ds(base + h * STEP, STEP), :] = jnp.concatenate(own, axis=0).astype(BF16)
            r_q = jnp.take_along_axis(rate_r[...], quad + lane_p // STEP, axis=1)
            w = jnp.exp(-r_q * (STEP - 1 - lane_p % STEP).astype(F32))
            t_li[pl.ds(base + 2 * STEP + h * poles, poles), :] = w.astype(BF16)
        index = j * gb + lane_p // width
        r_c = jnp.take_along_axis(rate_r[...], index, axis=1)
        s_c = jnp.take_along_axis(scale_r[...], index, axis=1)
        dec_step[:, lanes] = jnp.exp(-float(STEP) * r_c)
        dec_all[:, lanes] = jnp.exp(-float(rows) * r_c)
        diag = pole_p == lane_p % poles
        r_l = jnp.sum(jnp.where(diag, r_c, 0.0), axis=0, keepdims=True)
        s_l = jnp.sum(jnp.where(diag, s_c, 0.0), axis=0, keepdims=True)
        rate_l[:, lanes] = r_l
        scale_l[:, lanes] = s_l
        carry_w[0:STEP, lanes] = (s_l * jnp.exp(-r_l * (iota((STEP, LANES), 0) + 1).astype(F32))).astype(BF16)

    for k in range(2):
        widen(k)

        @pl.loop(k * blocks // 2, (k + 1) * blocks // 2)
        def _(j):
            tables(j)


    loads[4].wait()
    loads[5].wait()
    u_ext[TAPS:rows, :] = kb[: rows - TAPS, :] * vb[: rows - TAPS, :]
    loads[9].wait()
    loads[10].wait()

    group_w = (iota((STEP, rows // STEP * LANES), 1) % LANES) // width
    left_t = (iota((STEP, rows // STEP * LANES), 1) % LANES) < LANES // 2
    left_p = (iota((poles, rows // STEP * LANES), 1) % LANES) < LANES // 2
    quad_g = (iota((STEP, LANES), 1) // width) % QUAD
    pole_g = iota((poles, LANES), 1) // width

    def wait_pieces(sem, count):
        pltpu.make_async_copy(e_out.at[pl.ds(0, count)], s_in.at[pl.ds(0, count)], sem).wait()

    def piece(o):
        return pl.ds(pl.multiple_of(8 * lax.rem(o, 2), 8), 8), block(o // 2)

    def state_copy(o, frm):
        return pltpu.make_async_remote_copy(
            src_ref=s_loc.at[o], dst_ref=s_in.at[frm], send_sem=s_send, recv_sem=s_recv,
            device_id={"ctx": o}, device_id_type=MESH,
        )

    def short(j):
        lanes = block(j)
        at = pl.ds(pl.multiple_of(j * gb * STEP, gb * STEP), gb * STEP)
        rhs = jnp.concatenate([u_ext[a * STEP : a * STEP + window, lanes] for a in range(steps)], axis=1)
        res = jnp.dot(t_mr[at, 0:window], rhs, preferred_element_type=F32)
        conv = res[0:STEP]
        for g in range(1, gb):
            conv = jnp.where(group_w == g, res[g * STEP : (g + 1) * STEP], conv)
        diag = []
        for a in range(steps):
            part = pl.ds(a * STEP, STEP)
            out = (qb[part, lanes].astype(F32) * conv[:, a * LANES : (a + 1) * LANES]).astype(BF16)
            mr_h[part, lanes] = out
            u_li = klb[part, lanes] * out
            diag.append(jnp.concatenate([jnp.where(quad_g == r, u_li, jnp.zeros_like(u_li)) for r in range(QUAD)], axis=0))
        return jnp.concatenate(diag, axis=1)

    def long(j, diag):
        lanes = block(j)
        li_at = pl.ds(pl.multiple_of(j * 2 * (STEP + poles), 16), 2 * (STEP + poles))
        step_dec = dec_step[:, lanes]
        res = jnp.dot(t_li[li_at, :], diag, preferred_element_type=F32)
        own = jnp.where(left_t, res[0:STEP], res[STEP : 2 * STEP])
        ends = jnp.where(left_p, res[2 * STEP : 2 * STEP + poles], res[2 * STEP + poles :])
        state = None
        for a in range(steps):
            cut = slice(a * LANES, (a + 1) * LANES)
            near[pl.ds(a * STEP, STEP), lanes] = own[:, cut]
            if a == 0:
                state = ends[:, cut]
            else:
                s_part[a, :, lanes] = state
                state = state * step_dec + ends[:, cut]
        for h in range(2):
            s_loc[2 * j + h] = state[8 * h : 8 * h + 8].astype(BF16)

    def hand_out(j):
        for h in range(2):
            o = 2 * j + h

            @pl.when(o != me)
            def _():
                state_copy(o, me).start()

            @pl.when(o == me)
            def _():
                s_in[me] = s_loc[o]

    def enter_copy(owner, to):
        return pltpu.make_async_remote_copy(
            src_ref=e_out.at[to], dst_ref=e_loc.at[owner], send_sem=e_send, recv_sem=e_recv.at[owner // per_chunk],
            device_id={"ctx": to}, device_id_type=MESH,
        )

    def scan_owned():
        wait_pieces(s_recv, n - 1)
        my_a, my_b = piece(me)
        my_dec = dec_all[my_a, my_b]
        carried = jnp.zeros((8, LANES), F32)
        for b in range(n):
            e_out[b] = carried.astype(BF16)
            if b + 1 < n:
                carried = carried * my_dec + s_in[b].astype(F32)

        @pl.loop(1, n)
        def _(i):
            enter_copy(me, lax.rem(me + i, n)).start()

        e_loc[me] = e_out[me]

    @pl.loop(0, chunks)
    def _(c):
        halo(c).wait_recv()

        @pl.when(me == 0)
        def _():
            lanes = pl.ds(pl.multiple_of(c * cw, cw), cw)
            u_ext[0:TAPS, lanes] = jnp.zeros((TAPS, cw), BF16)

        js = [c * CHUNK_BLOCKS + i for i in range(CHUNK_BLOCKS)]
        diags = [short(j) for j in js]
        for j, diag in zip(js, diags):
            long(j, diag)
        @pl.when(c == 0)
        def _():
            widen(2)

        @pl.when(c == 1)
        def _():
            widen(3)
            for i in range(CHUNK_BLOCKS):
                hand_out(i)

        @pl.when(c > 0)
        def _():
            for j in js:
                hand_out(j)

    def spread_out(state):
        return jnp.concatenate([jnp.where(pole_g == g, state, jnp.zeros_like(state)) for g in range(gb)], axis=0)

    def from_own_states(j):
        lanes = block(j)
        diag = [spread_out(s_part[a, :, lanes].astype(BF16)) for a in range(1, steps)]
        add = jnp.dot(carry_w[0:STEP, lanes], jnp.concatenate(diag, axis=1), preferred_element_type=F32)
        for a in range(1, steps):
            near[pl.ds(a * STEP, STEP), lanes] += add[:, (a - 1) * LANES : a * LANES]
        pos = iota((rows - STEP, LANES), 0) + (STEP + 1)
        carry_w[STEP:, lanes] = (scale_l[:, lanes] * jnp.exp(-rate_l[:, lanes] * pos.astype(F32))).astype(BF16)

    scan_owned()

    @pl.loop(0, chunks)
    def _(c):
        for i in range(CHUNK_BLOCKS):
            from_own_states(c * CHUNK_BLOCKS + i)

    loads[11].wait()


    def finish(c):
        lanes = pl.ds(pl.multiple_of(c * cw, cw), cw)
        zero = jnp.zeros((LANES, LANES), BF16)
        a, b = [spread_out(jnp.concatenate([e_loc[2 * j], e_loc[2 * j + 1]], axis=0)) for j in (2 * c, 2 * c + 1)]
        diag = jnp.concatenate([jnp.concatenate([a, zero], axis=0), jnp.concatenate([zero, b], axis=0)], axis=1)
        for part in [pl.ds(i, 128) for i in range(0, rows, 128)]:
            far = jnp.dot(carry_w[part, lanes], diag, preferred_element_type=F32)
            li_h[part, lanes] = (qlb[part, lanes].astype(F32) * (near[part, lanes] + far)).astype(BF16)

    @pl.loop(0, chunks)
    def _(c):
        @pl.when(c == me // per_chunk)
        def _():
            wait_pieces(e_recv.at[c], per_chunk - 1)

        @pl.when(c != me // per_chunk)
        def _():
            wait_pieces(e_recv.at[c], per_chunk)

        finish(c)

    pltpu.make_async_copy(u_ext.at[pl.ds(rows, TAPS)], u_ext.at[pl.ds(0, TAPS)], h_send).wait()
    wait_pieces(s_send, n - 1)
    wait_pieces(e_send, n - 1)


def store(a_ref, b_ref, a_h, b_h, sem):
    size = a_ref.shape[0] // STORES
    copies = []
    for i in range(STORES):
        at = pl.ds(i * size, size)
        copies.append(pltpu.make_async_copy(a_ref.at[at], a_h.at[at], sem.at[2 * i]))
        copies.append(pltpu.make_async_copy(b_ref.at[at], b_h.at[at], sem.at[2 * i + 1]))
    for copy in copies:
        copy.start()
    for copy in copies:
        copy.wait()


def body(n, q, k, v, ql, kl, taps, rate, resid):
    rows, channels = q.shape
    groups, poles = rate.shape
    width = channels // groups
    blocks = channels // LANES
    chunks = blocks // CHUNK_BLOCKS
    assert n == 32 and taps.shape[1] == TAPS and 2 * blocks == n and width == poles == 16
    dma = pltpu.SemaphoreType.DMA
    vm = pltpu.VMEM
    hbm = pl.BlockSpec(memory_space=pltpu.HBM)
    small = pl.BlockSpec(memory_space=pltpu.VMEM)
    full = vm((rows, channels), BF16)
    out = jax.ShapeDtypeStruct((rows, channels), BF16)
    decays = vm((poles, channels), F32)
    states = vm((n, 8, LANES), BF16)
    results = pl.pallas_call(
        functools.partial(kernel, n, width, poles),
        out_shape=(out, out),
        in_specs=[hbm] * 8,
        out_specs=(small, small),
        scratch_shapes=[
            full, full, full, full, full,
            vm(taps.shape, BF16), vm((poles, groups), F32), vm((poles, groups), F32),
            vm((TAPS + rows, channels), BF16),
            vm((groups * STEP, 2 * LANES), BF16),
            vm((blocks * 2 * (STEP + poles), LANES), BF16),
            vm((rows, groups * poles), BF16),
            vm((rows, channels), F32),
            vm((rows // STEP, poles, channels), F32),
            states, states, states, states,
            vm((groups, LANES), F32), vm((groups, LANES), F32), vm((poles, groups), F32), vm((1, channels), F32), vm((1, channels), F32), decays, decays,
            pltpu.SemaphoreType.REGULAR((4,)), dma((12,)), dma(()), dma((chunks,)), dma(()), dma(()), dma(()), dma((chunks,)),
        ],
        compiler_params=pltpu.CompilerParams(collective_id=0, has_side_effects=True, vmem_limit_bytes=28 << 20),
        cost_estimate=pl.CostEstimate(flops=4 * 10**9, bytes_accessed=8 << 20, transcendentals=0),
    )(*[pltpu.with_memory_space_constraint(x, pltpu.HBM) for x in (q, k, v, ql, kl, taps, rate.T, resid.T)])
    return pl.pallas_call(
        store,
        out_shape=(out, out),
        in_specs=[small] * 2,
        out_specs=(hbm, hbm),
        scratch_shapes=[dma((2 * STORES,))],
        compiler_params=pltpu.CompilerParams(vmem_limit_bytes=4 << 20),
        cost_estimate=pl.CostEstimate(flops=0, bytes_accessed=4 << 20, transcendentals=0),
    )(*results)


def solution(mesh):
    rep_ctx = ("rep", "ctx")
    big = P(rep_ctx, "tp")
    return jax.shard_map(
        functools.partial(body, mesh.shape["ctx"]),
        mesh=mesh,
        in_specs=(big,) * 5 + (P("tp", None),) * 3,
        out_specs=(big, big),
        check_vma=False,
    )
```
